256 devices in a mesh: row: 4 (over x), col: 16 (over y, z_lo), gz: 4 (over z_hi, core).
Axes of the slice: x: 4, y: 4, z: 8 (z_hi: 2, z_lo: 4; z = z_hi * 4 + z_lo), core: 2. Of those that a mesh axis runs over, the one named last changes fastest.
Arguments:
- volume_field: bfloat16 [128, 32, 128, 512], P(None, 'row', 'col', 'gz'), may hold values from -6 to 6
- volume_load: bfloat16 [128, 32, 128, 512], P(None, 'row', 'col', 'gz'), may hold values from -6 to 6
- coefficient: float32 [32, 128, 512], P('row', 'col', 'gz'), may hold values from 0.25 to 2
- surface_block: bfloat16 [1024, 262144], P('row', 'col'), may hold values from -0.015625 to 0.015625
- trace_cell: int32 [4, 16, 4, 1024], P('row', 'col', 'gz'), may hold values from 0 to 8191, as said below
- flux_cell: int32 [4, 16, 4, 4], P('row', 'col', 'gz'), may hold values from 0 to 8191, as said below
Outputs:
- new_field: bfloat16 [128, 32, 128, 512], P(None, 'row', 'col', 'gz')
- surface_flux: float32 [128, 1024], P('gz', ('row', 'col'))
The draws below stay inside these ranges and needn't reach their ends.
Inputs may be any that keep to these rules, and one draw needn't show every extreme that they name: `trace_cell`: within each device's 1024 entries, entry values are local cell numbers, one from each aligned run of 8 consecutive cells, in a permuted order; the first and last cells of the block are always chosen. `flux_cell`: within each device's 4 entries, entry values are local cell numbers, one from each aligned run of 2048 consecutive cells, in a permuted order; the first and last cells of the block are always chosen.
All inputs are finite; a program needn't handle non-finite values.
Results may differ from the reference program's by a relative error of at most 0.0032.
Values may be sent and summed in bfloat16 or wider, within the bound.
A program may use at most 128 MiB of HBM per device.

```python
import jax
import jax.numpy as jnp
from jax import lax

RHS = 128
VX = 8
VY = 8
VZ = 128
TS = 1024
NS = 262144
NSR = 1024
FS = 4
NX = 32
NY = 128
NZ = 512
N_ROW = 4
N_COL = 16
N_GZ = 4


def spread_cells(key, per_device):
    device_count = N_ROW * N_COL * N_GZ
    stride = VX * VY * VZ // per_device
    offsets = jax.random.randint(key, (device_count, per_device), 0, stride, dtype=jnp.int32)
    column = jnp.arange(per_device, dtype=jnp.int32)[None, :]
    offsets = jnp.where(column == 0, 0, jnp.where(column == per_device - 1, stride - 1, offsets))
    chosen_cells = column * stride + offsets
    sub_keys = jax.random.split(jax.random.fold_in(key, 5), device_count)
    shuffle = jax.vmap(lambda sub: jax.random.permutation(sub, per_device))(sub_keys)
    chosen_cells = jnp.take_along_axis(chosen_cells, shuffle.astype(jnp.int32), axis=1)
    return chosen_cells.reshape(N_ROW, N_COL, N_GZ, per_device).astype(jnp.int32)


def draw_trace_cell(key, part):
    return spread_cells(jax.random.fold_in(key, 11), TS)


def draw_flux_cell(key, part):
    return spread_cells(jax.random.fold_in(key, 23), FS)


def with_spikes(values, own_key, source, target, blocks, factor):
    def block_of(position):
        return (jnp.arange(values.shape[position]) // (values.shape[position] // blocks)).reshape((-1,) + (1,) * (values.ndim - 1 - position))

    first = jax.random.permutation(own_key, blocks)[block_of(target)]
    far = (block_of(target) + blocks // 2) % blocks
    return jnp.where((block_of(source) == first) | (block_of(source) == far), factor * values, values)


def block_scale(own_key, extent, shards, low, top_value):
    level = 1.0
    for dim, parts in shards:
        draws = jax.random.uniform(jax.random.fold_in(jax.random.fold_in(own_key, 6), dim), (parts,), jnp.float32, low / len(shards), top_value / len(shards))
        level = level * jnp.repeat(jnp.exp(draws), extent[dim] // parts).reshape((-1,) + (1,) * (len(extent) - 1 - dim))
    return level


def centred(rng, shape, width, most, shards=(), held_as=jnp.bfloat16):
    entries = width * jax.random.normal(rng, shape, jnp.float32)
    if shards:
        entries = entries * block_scale(rng, shape, shards, -0.22, 0.18)
    return jnp.clip(entries, -most, most).astype(held_as)


def noise_with(key, shape, deviation, most, cuts, heavy, held_as=jnp.bfloat16):
    entries = deviation * jax.random.normal(key, shape, jnp.float32)
    if cuts:
        entries = entries * block_scale(key, shape, cuts, -0.22, 0.18)
    return jnp.clip(with_spikes(entries, jax.random.fold_in(key, 3), *heavy), -most, most).astype(held_as)


def setup_inputs(seed: int = 0) -> dict:
    splits = jax.random.split(jax.random.key(seed), 7)
    return {
        "volume_field": centred(splits[0], (RHS, NX, NY, NZ), 1.0, 6.0, ((1, 4), (2, 16), (3, 4))),
        "volume_load": centred(splits[1], (RHS, NX, NY, NZ), 1.0, 6.0, ((1, 4), (2, 16), (3, 4))),
        "coefficient": jnp.clip(0.25 + 1.75 * jax.random.uniform(splits[2], (NX, NY, NZ), jnp.float32) ** block_scale(splits[2], (NX, NY, NZ), ((0, 4), (1, 16), (2, 4)), -0.2, 0.2), 0.25, 2.0),
        "surface_block": noise_with(splits[3], (NSR, NS), NS ** -0.5, 0.015625, ((0, 4), (1, 16)), (1, 0, 16, 2.0)),
        "trace_cell": draw_trace_cell(jax.random.fold_in(splits[6], 71), 0),
        "flux_cell": draw_flux_cell(jax.random.fold_in(splits[6], 71), 0),
    }


OMEGA = 0.8


def relax(current, source, diagonal):
    centre = current.astype(jnp.float32)
    padded = jnp.pad(centre, 1)
    beside = padded[2:, 1:-1, 1:-1] + padded[:-2, 1:-1, 1:-1]
    beside = beside + padded[1:-1, 2:, 1:-1] + padded[1:-1, :-2, 1:-1]
    beside = beside + padded[1:-1, 1:-1, 2:] + padded[1:-1, 1:-1, :-2]
    return (centre + OMEGA * (source - (diagonal * centre - beside)) / diagonal).astype(jnp.bfloat16)


def reference(volume_field, volume_load, coefficient, surface_block, trace_cell, flux_cell):
    cell_count = VX * VY * VZ
    blocks = volume_field.reshape(RHS, N_ROW, VX, N_COL, VY, N_GZ, VZ)
    blocks = blocks.transpose(0, 1, 3, 5, 2, 4, 6).reshape(RHS, N_ROW, N_COL, N_GZ, cell_count)
    indices = jnp.broadcast_to(trace_cell[None].astype(jnp.int32), (RHS, N_ROW, N_COL, N_GZ, TS))
    traced = jnp.take_along_axis(blocks, indices, axis=4)
    trace_values = traced.transpose(0, 2, 1, 3, 4).reshape(RHS, N_COL * N_ROW * N_GZ * TS)
    surface_flux = jnp.dot(trace_values, surface_block.T, preferred_element_type=jnp.float32)
    flux_parts = surface_flux.reshape(RHS, N_ROW, N_COL, N_GZ, FS).astype(jnp.float32)
    onehot = (flux_cell[..., None].astype(jnp.int32) == jnp.arange(cell_count, dtype=jnp.int32)).astype(jnp.float32)
    placed = jnp.einsum('srcgk,rcgkv->srcgv', flux_parts, onehot, precision=lax.Precision.HIGHEST)
    placed = placed.reshape(RHS, N_ROW, N_COL, N_GZ, VX, VY, VZ).transpose(0, 1, 4, 2, 5, 3, 6)
    placed = placed.reshape(RHS, NX, NY, NZ)
    diagonal = 6.0 + coefficient.astype(jnp.float32)

    def one_side(items):
        current, load_term, extra = items
        source = load_term.astype(jnp.float32) + extra
        for repeat in range(3):
            current = relax(current, source, diagonal)
        return current

    new_field = lax.map(one_side, (volume_field, volume_load, placed))
    return new_field, surface_flux
```

```python
import functools

import jax
import jax.numpy as jnp
from jax import lax
from jax.experimental import pallas as pl
from jax.experimental.pallas import tpu as pltpu
from jax.sharding import PartitionSpec as P

MESH = pl.DeviceIdType.MESH
BF = jnp.bfloat16
F32 = jnp.float32
I32 = jnp.int32
OMEGA = 0.8
GROUPS = 4
BATCH = 8
NB = GROUPS * BATCH
OFFS = ((-1, 0, 0), (1, 0, 0), (0, -1, 0), (0, 1, 0), (0, 0, -1), (0, 0, 1))


def iota(shape, dim):
    return lax.broadcasted_iota(I32, shape, dim)


def onehot(cond):
    return jnp.where(cond, 1.0, 0.0).astype(BF)


def nt(a, b, **kw):
    return lax.dot_general(a, b, (((1,), (1,)), ((), ())), preferred_element_type=F32, **kw)


def tn(a, b):
    return lax.dot_general(a, b, (((0,), (0,)), ((), ())), preferred_element_type=F32)


def mm(a, b):
    return jnp.dot(a, b, preferred_element_type=F32)


def kernel(
    field_hbm, load_hbm, coef_ref, sb_hbm, tcell_ref, fcell_ref,
    out_hbm, flux_ref,
    v0, ld, v1, v2, v3, sb, tr, w4, hb, fs, zh, zs,
    abd, hbd, ebd, smat, gmat, rmat, wz, m4, cbuf, c2, pbuf,
    part, cown, csend, crecv, qbuf, yrecv, zsend, zrecv, fbuf, fall,
    gbuf, gnb, cinfo, cnb, lmask, zmask, val, val3,
    insem, sbsem, outsem, hs_s, hs_r, ts_s, ts_r, c_s, c_r, y_s, y_r, z_s, z_r,
    f_s, f_r, g_s, g_r, i_s, i_r,
):
    r = lax.axis_index("row")
    c = lax.axis_index("col")
    g = lax.axis_index("gz")
    y, zl = c // 4, c % 4
    zhi, b = g // 2, g % 2
    right, left, far = (r + 1) % 4, (r + 3) % 4, (r + 2) % 4
    jz = zl * 2 + zhi

    exists = (r > 0, r < 3, c > 0, c < 15, g > 0, g < 3)
    nbid = ({"row": r - 1}, {"row": r + 1}, {"col": c - 1}, {"col": c + 1}, {"gz": g - 1}, {"gz": g + 1})

    def rcopy(src, dst, ss, rs, dev):
        return pltpu.make_async_remote_copy(
            src_ref=src, dst_ref=dst, send_sem=ss, recv_sem=rs, device_id=dev, device_id_type=MESH
        )

    barrier = pltpu.get_barrier_semaphore()

    def greet(dev):
        pl.semaphore_signal(barrier, inc=1, device_id=dev, device_id_type=MESH)

    def zdev(o):
        j = (jz + o) % 8
        return {"col": y * 4 + j // 2, "gz": (j % 2) * 2 + b}

    for o in range(1, 4):
        greet({"row": (r + o) % 4})
        greet({"col": ((y + o) % 4) * 4 + zl})
    for o in range(1, 8):
        greet(zdev(o))
    greet({"gz": zhi * 2 + 1 - b})
    greet({"gz": (1 - zhi) * 2 + 1 - b})
    wraps = ((zl == 0) & (c > 0), (zl == 3) & (c < 15))
    for d in range(2):
        @pl.when(wraps[d])
        def _(d=d):
            greet(nbid[2 + d])
    peers = 15 + jnp.where(wraps[0], 1, 0) + jnp.where(wraps[1], 1, 0)

    cin = []
    for k in range(GROUPS):
        rows = pl.ds(k * 2048, 2048)
        cp = pltpu.make_async_copy(field_hbm.at[rows], v0.at[rows], insem.at[0, k])
        cp.start()
        cin.append(cp)
    csb = []
    for o in range(4):
        cols = pl.multiple_of((((r + o) % 4) * 4 + g) * 1024, 1024)
        cp = pltpu.make_async_copy(sb_hbm.at[:, pl.ds(cols, 1024)], sb.at[o], sbsem.at[o])
        cp.start()
        csb.append(cp)
    cld = []
    for k in range(GROUPS):
        rows = pl.ds(k * 2048, 2048)
        cp = pltpu.make_async_copy(load_hbm.at[rows], ld.at[rows], insem.at[1, k])
        cp.start()
        cld.append(cp)

    cell = tcell_ref[...]
    chosen_xy = onehot((cell >> 7) == iota((64, 1024), 0))
    chosen_z = onehot((cell & 127) == iota((128, 1024), 0))
    mask = nt(chosen_xy, chosen_z).astype(BF)
    for k in range(4):
        m4[k * 64:(k + 1) * 64, :] = mask
    gmat[...] = onehot((iota((128, 128), 0) >> 3) == (iota((128, 128), 1) & 15))
    rmat[...] = onehot(iota((32, 256), 0) == (iota((32, 256), 1) >> 3))

    @pl.loop(0, 8)
    def _(k):
        rows = pl.ds(pl.multiple_of(k * 128, 128), 128)
        pbuf[rows, :] = onehot((cell >> 3) == iota((128, 1024), 0) + k * 128)

    for k in range(GROUPS):
        cin[k].wait()

        @pl.loop(k * BATCH, (k + 1) * BATCH)
        def _(q):
            rows = pl.ds(pl.multiple_of(q * 256, 256), 256)
            t = mm(v0[rows, :] * m4[...], gmat[...])
            same = (iota((256, 128), 0) & 7) == (iota((256, 128), 1) >> 4)
            t = jnp.where(same, t, 0.0).astype(BF)
            cbuf[pl.ds(pl.multiple_of(q * 32, 32), 32), :] = mm(rmat[...], t)

    for x in range(8):
        c2[:, x * 128:(x + 1) * 128] = cbuf[pl.ds(x, 128, stride=8), :].astype(BF)
    for h in range(2):
        tr[r, h] = mm(c2[...], pbuf[:, h * 512:(h + 1) * 512]).astype(BF)

    pl.semaphore_wait(barrier, peers)

    to_right = [rcopy(tr.at[r, h], tr.at[r, h], ts_s.at[0, h], ts_r.at[0, h], {"row": right}) for h in range(2)]
    to_left = [rcopy(tr.at[r, h], tr.at[r, h], ts_s.at[1, h], ts_r.at[1, h], {"row": left}) for h in range(2)]
    from_left = [rcopy(tr.at[left, h], tr.at[left, h], ts_s.at[0, h], ts_r.at[0, h], {"row": right}) for h in range(2)]
    from_right = [rcopy(tr.at[right, h], tr.at[right, h], ts_s.at[1, h], ts_r.at[1, h], {"row": left}) for h in range(2)]
    relay_right = rcopy(tr.at[left, 0], tr.at[left, 0], ts_s.at[2, 0], ts_r.at[2, 0], {"row": right})
    relay_left = rcopy(tr.at[right, 1], tr.at[right, 1], ts_s.at[2, 1], ts_r.at[2, 1], {"row": left})
    from_far = [
        rcopy(tr.at[far, 0], tr.at[far, 0], ts_s.at[2, 0], ts_r.at[2, 0], {"row": right}),
        rcopy(tr.at[far, 1], tr.at[far, 1], ts_s.at[2, 1], ts_r.at[2, 1], {"row": left}),
    ]
    to_right[0].start()
    to_left[1].start()
    to_right[1].start()
    to_left[0].start()

    p, q = iota((128, 256), 0), iota((128, 256), 1)
    d, o = p >> 5, p & 7
    qx, qy = (q >> 3) & 7, q & 7
    hit = jnp.where(
        d < 2,
        jnp.where(qx == d * 7, jnp.where(qy == o, 1.0, 0.0), 0.0),
        jnp.where(qy == (d - 2) * 7, jnp.where(qx == o, 1.0, 0.0), 0.0),
    )
    ebd[...] = jnp.where(((p >> 3) & 3) == (q >> 6), hit, 0.0).astype(BF)
    p, q = iota((256, 128), 0), iota((256, 128), 1)
    d, o = q >> 5, q & 7
    px, py = (p >> 3) & 7, p & 7
    hit = jnp.where(
        d < 2,
        jnp.where(px == d * 7, jnp.where(py == o, 1.0, 0.0), 0.0),
        jnp.where(py == (d - 2) * 7, jnp.where(px == o, 1.0, 0.0), 0.0),
    )
    hbd[...] = jnp.where(((q >> 3) & 3) == (p >> 6), hit, 0.0).astype(BF)
    p, q = iota((256, 256), 0), iota((256, 256), 1)
    dx = jnp.abs(((p >> 3) & 7) - ((q >> 3) & 7))
    dy = jnp.abs((p & 7) - (q & 7))
    abd[...] = jnp.where((p >> 6) == (q >> 6), jnp.where(dx + dy == 1, 1.0, 0.0), 0.0).astype(BF)
    smat[...] = onehot(jnp.abs(iota((128, 128), 0) - iota((128, 128), 1)) == 1)
    wz[...] = onehot(iota((16, 128), 1) == jnp.where(iota((16, 128), 0) < 2, iota((16, 128), 0) * 127, -1))

    w = OMEGA / (6.0 + coef_ref[...])
    for k in range(4):
        w4[k * 64:(k + 1) * 64, :] = w

    row8 = iota((8, 128), 0) & 3
    cells = jnp.zeros((8, 128), I32)
    weight = jnp.zeros((8, 128), F32)
    number = iota((64, 128), 0) * 128 + iota((64, 128), 1)
    for k in range(4):
        fc = fcell_ref[k]
        wk = jnp.sum(jnp.where(number == fc, w, 0.0), axis=(0, 1), keepdims=True)
        cells = jnp.where(row8 == k, fc, cells)
        weight = jnp.where(row8 == k, wk, weight)
    cinfo[...] = cells.astype(F32)
    for d in range(6):
        @pl.when(exists[d])
        def _(d=d):
            rcopy(cinfo, cnb.at[d ^ 1], i_s.at[d], i_r.at[d ^ 1], nbid[d]).start()

    for d in range(6):
        @pl.when(jnp.logical_not(exists[d]))
        def _(d=d):
            cnb[d] = jnp.zeros((8, 128), F32)
            gnb[d] = jnp.zeros((8, 128), F32)
            for s in range(3):
                if d < 4:
                    @pl.loop(0, 8)
                    def _(k, s=s):
                        hb[s, d, pl.ds(pl.multiple_of(k * 128, 128), 128), :] = jnp.zeros((128, 128), BF)
                else:
                    zh[s, d - 4] = jnp.zeros((NB, 256), F32)

    def halo(s, d, k):
        if d < 4:
            rows = pl.ds(pl.multiple_of(k * 256, 256), 256)
            src, dst = fs.at[s, d, rows], hb.at[s, d ^ 1, rows]
        else:
            rows = pl.ds(pl.multiple_of(k * 8, 8), 8)
            src, dst = zs.at[s, d - 4, rows], zh.at[s, (d ^ 1) - 4, rows]
        return rcopy(src, dst, hs_s.at[s, d, k], hs_r.at[s, d ^ 1, k], nbid[d])

    def send_halos(s, k):
        for d in (2, 3, 0, 1, 4, 5):
            @pl.when(exists[d])
            def _(d=d):
                halo(s, d, k).start()

    def wait_halos(s, k):
        for d in range(6):
            @pl.when(exists[d])
            def _(d=d):
                if d < 4:
                    rows = pl.ds(pl.multiple_of(k * 256, 256), 256)
                    dst = hb.at[s, d, rows]
                else:
                    rows = pl.ds(pl.multiple_of(k * 8, 8), 8)
                    dst = zh.at[s, d - 4, rows]
                rcopy(dst, dst, hs_s.at[s, d, k], hs_r.at[s, d, k], nbid[d]).wait_recv()

    def faces(s, q, v):
        f = mm(ebd[...], v).astype(BF)
        rows = pl.ds(pl.multiple_of(q * 32, 32), 32)
        for d in range(4):
            fs[s, d, rows, :] = f[d * 32:(d + 1) * 32, :]
        zf = nt(wz[...], v)
        for d in range(2):
            zs[s, d, pl.ds(q, 1), :] = zf[d:d + 1, :]

    def sweep(s, q, vin, extra_rows, extra_cols):
        rows = pl.ds(pl.multiple_of(q * 256, 256), 256)
        hrows = pl.ds(pl.multiple_of(q * 32, 32), 32)
        v = vin[rows, :]
        around = jnp.concatenate([hb[s, d, hrows, :] for d in range(4)], axis=0)
        rid = iota((16, 256), 0)
        zz = jnp.where(rid == 0, zh[s, 0, pl.ds(q, 1), :], jnp.where(rid == 1, zh[s, 1, pl.ds(q, 1), :], 0.0))
        lhs, rhs = zz.astype(BF), wz[...]
        if extra_rows is not None:
            lhs = jnp.concatenate([lhs, extra_rows], axis=0)
            rhs = jnp.concatenate([rhs, extra_cols], axis=0)
        acc = mm(abd[...], v) + mm(hbd[...], around) + mm(v, smat[...]) + tn(lhs, rhs)
        return 0.2 * v.astype(F32) + w4[...] * (ld[rows, :].astype(F32) + acc)

    def spread(q, values, places):
        pick = onehot(iota((128, 256), 0) == 4 * q + (iota((128, 256), 1) >> 6))
        return (mm(values, pick) * places).astype(BF)

    def sweep1(k):
        wait_halos(0, k)

        @pl.loop(k * BATCH, (k + 1) * BATCH)
        def _(q):
            new = sweep(0, q, v0, None, None).astype(BF)
            v1[pl.ds(pl.multiple_of(q * 256, 256), 256), :] = new
            faces(1, q, new)
        send_halos(1, k)

    for k in range(GROUPS):
        @pl.loop(k * BATCH, (k + 1) * BATCH)
        def _(q):
            faces(0, q, v0[pl.ds(pl.multiple_of(q * 256, 256), 256), :])
        send_halos(0, k)
        if k == 1:
            from_left[0].wait_recv()
            relay_right.start()
            from_right[1].wait_recv()
            relay_left.start()

    for k in range(GROUPS):
        cld[k].wait()

    def product(o):
        csb[o].wait()
        src = (r + o) % 4
        return nt(sb[o, :, 0:512], tr[src, 0]) + nt(sb[o, :, 512:1024], tr[src, 1])

    part[...] = product(0)
    from_left[1].wait_recv()
    part[...] += product(3)
    from_right[0].wait_recv()
    part[...] += product(1)
    sweep1(0)
    from_far[0].wait_recv()
    from_far[1].wait_recv()
    total = (part[...] + product(2)).reshape(32, 8, 128)
    low, high = total[:, 0:4, :], total[:, 4:8, :]
    first = b == 0
    cown[...] = jnp.where(first, low, high)
    csend[...] = jnp.where(first, high, low)
    core = rcopy(csend, crecv, c_s, c_r, {"gz": g + 1 - 2 * b})
    core.start()
    sweep1(1)
    core.wait_recv()
    qbuf[...] = cown[...] + crecv[...]
    yrecv[y] = qbuf[pl.ds(y * 8, 8)]
    ycopies = []
    for o in range(1, 4):
        peer = (y + o) % 4
        cp = rcopy(qbuf.at[pl.ds(peer * 8, 8)], yrecv.at[y], y_s.at[o - 1], y_r.at[o - 1], {"col": peer * 4 + zl})
        cp.start()
        ycopies.append(cp)
    sweep1(2)
    for o in range(1, 4):
        peer = (y + 4 - o) % 4
        rcopy(yrecv.at[peer], yrecv.at[peer], y_s.at[o - 1], y_r.at[o - 1], {"col": peer * 4 + zl}).wait_recv()
    zsend[...] = (yrecv[0] + yrecv[1]) + (yrecv[2] + yrecv[3])
    zrecv[jz] = zsend[jz]
    zcopies = []
    for o in range(1, 8):
        peer = (jz + o) % 8
        cp = rcopy(zsend.at[peer], zrecv.at[jz], z_s.at[o - 1], z_r.at[o - 1], zdev(o))
        cp.start()
        zcopies.append(cp)
    sweep1(3)

    for d in range(6):
        @pl.when(exists[d])
        def _(d=d):
            rcopy(cnb.at[d], cnb.at[d], i_s.at[d], i_r.at[d], nbid[d]).wait_recv()
    mine = iota((8, 128), 0) < 4
    lane = iota((8, 256), 1) & 63
    for k in range(7):
        if k == 0:
            tx, ty, tz = cells >> 10, (cells >> 7) & 7, cells & 127
        else:
            ox, oy, oz = OFFS[k - 1]
            other = cnb[k - 1].astype(I32)
            at = jnp.where(mine, cells, other)
            tx = (at >> 10) + jnp.where(mine, ox, 7 * ox)
            ty = ((at >> 7) & 7) + jnp.where(mine, oy, 7 * oy)
            tz = (at & 127) + jnp.where(mine, oz, 127 * oz)
        txy = jnp.where((tx >= 0) & (tx < 8) & (ty >= 0) & (ty < 8), tx * 8 + ty, -1)
        tz = jnp.where((tz >= 0) & (tz < 128), tz, -1)
        spots = jnp.where(jnp.concatenate([txy, txy], axis=1) == lane, 1.0, 0.0)
        cols = jnp.where(tz == iota((8, 128), 1), 1.0, 0.0)
        for part_ in range(2):
            lmask[part_ * 56 + k * 8:part_ * 56 + k * 8 + 8, :] = spots
            zmask[part_ * 56 + k * 8:part_ * 56 + k * 8 + 8, :] = cols

    for o in range(1, 8):
        peer = (jz + 8 - o) % 8
        rcopy(zrecv.at[peer], zrecv.at[peer], z_s.at[o - 1], z_r.at[o - 1], zdev(8 - o)).wait_recv()
    own = zrecv[0]
    for j in range(1, 8):
        own = own + zrecv[j]
    fbuf[...] = own
    own8 = jnp.concatenate([own, own], axis=0)
    gvals = weight * own8
    gbuf[...] = gvals
    for d in range(6):
        @pl.when(exists[d])
        def _(d=d):
            rcopy(gbuf, gnb.at[d ^ 1], g_s.at[d], g_r.at[d ^ 1], nbid[d]).start()
    fall[g] = own
    fcopies = []
    for o in range(1, 4):
        cp = rcopy(fbuf, fall.at[g], f_s.at[o - 1], f_r.at[o - 1], {"gz": (g + o) % 4})
        cp.start()
        fcopies.append(cp)

    for d in range(6):
        @pl.when(exists[d])
        def _(d=d):
            rcopy(gnb.at[d], gnb.at[d], g_s.at[d], g_r.at[d], nbid[d]).wait_recv()

    def split(values):
        hi = values.astype(BF).astype(F32)
        return hi, values - hi

    centre = jnp.where(mine, own8, 0.0)
    pieces = [1.2 * centre] + [jnp.where(mine, gvals, gnb[d]) for d in range(6)]
    for k in range(7):
        hi, lo = split(pieces[k])
        val[k * 8:k * 8 + 8, :] = hi
        val[56 + k * 8:56 + k * 8 + 8, :] = lo
    hi, lo = split(centre)
    val3[0:8, :] = hi
    val3[8:16, :] = lo

    @pl.loop(0, GROUPS)
    def _(k):
        wait_halos(1, k)

        @pl.loop(k * BATCH, (k + 1) * BATCH)
        def _(q):
            rows = spread(q, val[...].astype(BF), lmask[...])
            new = sweep(1, q, v1, rows, zmask[...].astype(BF)).astype(BF)
            v2[pl.ds(pl.multiple_of(q * 256, 256), 256), :] = new
            faces(2, q, new)
        send_halos(2, k)

    def put(k):
        rows = pl.ds(pl.multiple_of(k * 2048, 2048), 2048)
        return pltpu.make_async_copy(v3.at[rows], out_hbm.at[rows], outsem.at[k])

    @pl.loop(0, GROUPS)
    def _(k):
        wait_halos(2, k)

        @pl.loop(k * BATCH, (k + 1) * BATCH)
        def _(q):
            places = jnp.concatenate([lmask[0:8, :], lmask[0:8, :]], axis=0)
            cols = jnp.concatenate([zmask[0:8, :], zmask[0:8, :]], axis=0).astype(BF)
            rows = spread(q, val3[...].astype(BF), places)
            new = sweep(2, q, v2, rows, cols).astype(BF)
            v3[pl.ds(pl.multiple_of(q * 256, 256), 256), :] = new
        put(k).start()

    for o in range(1, 4):
        peer = (g + 4 - o) % 4
        rcopy(fall.at[peer], fall.at[peer], f_s.at[o - 1], f_r.at[o - 1], {"gz": peer}).wait_recv()
    sel = jnp.where(iota((32, 128), 1) == g * 32 + iota((32, 128), 0), 1.0, 0.0)
    rows16 = jnp.concatenate([fall[0], fall[1], fall[2], fall[3]], axis=0)
    flux_ref[...] = nt(sel, rows16, precision=lax.Precision.HIGHEST)

    for cp in to_right + to_left + [relay_right, relay_left, core] + ycopies + zcopies + fcopies:
        cp.wait_send()
    for d in range(6):
        @pl.when(exists[d])
        def _(d=d):
            rcopy(cinfo, cnb.at[d ^ 1], i_s.at[d], i_r.at[d ^ 1], nbid[d]).wait_send()
            rcopy(gbuf, gnb.at[d ^ 1], g_s.at[d], g_r.at[d ^ 1], nbid[d]).wait_send()
            for s in range(3):
                @pl.loop(0, GROUPS)
                def _(k):
                    halo(s, d, k).wait_send()
    for k in range(GROUPS):
        put(k).wait()


def per_device(volume_field, volume_load, coefficient, surface_block, trace_cell, flux_cell):
    side_count, first_span, second_span, third_span = volume_field.shape
    rows = side_count * first_span * second_span
    vm = pltpu.VMEM
    dma = pltpu.SemaphoreType.DMA
    scratch = [
        vm((rows, 128), BF), vm((rows, 128), BF), vm((rows, 128), BF), vm((rows, 128), BF), vm((rows, 128), BF),
        vm((4, 256, 1024), BF), vm((4, 2, 128, 512), BF), vm((256, 128), F32),
        vm((3, 4, 1024, 128), BF), vm((3, 4, 1024, 128), BF), vm((3, 2, NB, 256), F32), vm((3, 2, NB, 256), F32),
        vm((256, 256), BF), vm((256, 128), BF), vm((128, 256), BF), vm((128, 128), BF), vm((128, 128), BF),
        vm((32, 256), BF), vm((16, 128), BF), vm((256, 128), BF), vm((1024, 128), F32), vm((128, 1024), BF),
        vm((1024, 1024), BF),
        vm((256, 128), F32), vm((32, 4, 128), F32), vm((32, 4, 128), F32), vm((32, 4, 128), F32),
        vm((32, 4, 128), F32), vm((4, 8, 4, 128), F32), vm((8, 4, 128), F32), vm((8, 4, 128), F32),
        vm((4, 128), F32), vm((4, 4, 128), F32),
        vm((8, 128), F32), vm((6, 8, 128), F32), vm((8, 128), F32), vm((6, 8, 128), F32),
        vm((112, 256), F32), vm((112, 128), F32), vm((112, 128), F32), vm((16, 128), F32),
        dma((2, GROUPS)), dma((4,)), dma((GROUPS,)), dma((3, 6, GROUPS)), dma((3, 6, GROUPS)),
        dma((3, 2)), dma((3, 2)), dma, dma, dma((3,)), dma((3,)), dma((7,)), dma((7,)),
        dma((3,)), dma((3,)), dma((6,)), dma((6,)), dma((6,)), dma((6,)),
    ]
    anywhere = pl.BlockSpec(memory_space=pl.ANY)
    local = pl.BlockSpec(memory_space=pltpu.VMEM)
    new_field, surface_flux = pl.pallas_call(
        kernel,
        out_shape=(jax.ShapeDtypeStruct((rows, 128), BF), jax.ShapeDtypeStruct((32, 16), F32)),
        in_specs=[anywhere, anywhere, local, anywhere, local, pl.BlockSpec(memory_space=pltpu.SMEM)],
        out_specs=(anywhere, local),
        scratch_shapes=scratch,
        compiler_params=pltpu.CompilerParams(
            collective_id=0, has_side_effects=True, vmem_limit_bytes=60 * 1024 * 1024
        ),
    )(
        volume_field.reshape(rows, 128),
        volume_load.reshape(rows, 128),
        coefficient.reshape(64, 128),
        surface_block,
        trace_cell.reshape(1, 1024),
        flux_cell.reshape(4),
    )
    return new_field.reshape(volume_field.shape), surface_flux


def solution(mesh):
    in_specs = (
        P(None, "row", "col", "gz"),
        P(None, "row", "col", "gz"),
        P("row", "col", "gz"),
        P("row", "col"),
        P("row", "col", "gz", None),
        P("row", "col", "gz", None),
    )
    out_specs = (P(None, "row", "col", "gz"), P("gz", ("row", "col")))
    return jax.shard_map(
        per_device, mesh=mesh, in_specs=in_specs, out_specs=out_specs, check_vma=False
    )
```

```python
import functools

import jax
import jax.numpy as jnp
from jax import lax
from jax.experimental import pallas as pl
from jax.experimental.pallas import tpu as pltpu
from jax.sharding import PartitionSpec as P

MESH = pl.DeviceIdType.MESH
BF = jnp.bfloat16
F32 = jnp.float32
I32 = jnp.int32
OMEGA = 0.8
GROUPS = 4
UNITS = 4
STEP = 2
NB = GROUPS * UNITS * 2
OFFS = ((-1, 0, 0), (1, 0, 0), (0, -1, 0), (0, 1, 0), (0, 0, -1), (0, 0, 1))


def iota(shape, dim):
    return lax.broadcasted_iota(I32, shape, dim)


def onehot(cond):
    return jnp.where(cond, 1.0, 0.0).astype(BF)


def nt(a, b, **kw):
    return lax.dot_general(a, b, (((1,), (1,)), ((), ())), preferred_element_type=F32, **kw)


def tn(a, b):
    return lax.dot_general(a, b, (((0,), (0,)), ((), ())), preferred_element_type=F32)


def mm(a, b):
    return jnp.dot(a, b, preferred_element_type=F32)


def kernel(
    field_hbm, load_hbm, coef_ref, sb_hbm, tcell_ref, fcell_ref,
    out_hbm, flux_ref,
    v0, ld, v1, v2, v3, sb, tr, w4, hb, fs, zh, zs,
    ah, emat, ss, gg, rmat, wz, uu, m4, ymask, cbuf, c2, pbuf,
    part, cown, csend, crecv, qbuf, yrecv, zsend, zrecv, fbuf, fall,
    gbuf, gnb, cinfo, cnb, lmask, zcols, zcols3, val, val3,
    insem, sbsem, outsem, hs_s, hs_r, ts_s, ts_r, c_s, c_r, y_s, y_r, z_s, z_r,
    f_s, f_r, g_s, g_r, i_s, i_r,
):
    r = lax.axis_index("row")
    c = lax.axis_index("col")
    g = lax.axis_index("gz")
    y, zl = c // 4, c % 4
    zhi, b = g // 2, g % 2
    right, left, far = (r + 1) % 4, (r + 3) % 4, (r + 2) % 4
    jz = zl * 2 + zhi

    exists = (r > 0, r < 3, c > 0, c < 15, g > 0, g < 3)
    nbid = ({"row": r - 1}, {"row": r + 1}, {"col": c - 1}, {"col": c + 1}, {"gz": g - 1}, {"gz": g + 1})

    def rcopy(src, dst, ss, rs, dev):
        return pltpu.make_async_remote_copy(
            src_ref=src, dst_ref=dst, send_sem=ss, recv_sem=rs, device_id=dev, device_id_type=MESH
        )

    barrier = pltpu.get_barrier_semaphore()

    def greet(dev):
        pl.semaphore_signal(barrier, inc=1, device_id=dev, device_id_type=MESH)

    def zdev(o):
        j = (jz + o) % 8
        return {"col": y * 4 + j // 2, "gz": (j % 2) * 2 + b}

    for o in range(1, 4):
        greet({"row": (r + o) % 4})
        greet({"col": ((y + o) % 4) * 4 + zl})
    for o in range(1, 8):
        greet(zdev(o))
    greet({"gz": zhi * 2 + 1 - b})
    greet({"gz": (1 - zhi) * 2 + 1 - b})
    wraps = ((zl == 0) & (c > 0), (zl == 3) & (c < 15))
    for d in range(2):
        @pl.when(wraps[d])
        def _(d=d):
            greet(nbid[2 + d])
    peers = 15 + jnp.where(wraps[0], 1, 0) + jnp.where(wraps[1], 1, 0)

    cin = []
    for k in range(GROUPS):
        rows = pl.ds(k * 2048, 2048)
        cp = pltpu.make_async_copy(field_hbm.at[rows], v0.at[rows], insem.at[0, k])
        cp.start()
        cin.append(cp)
    csb = []
    for o in range(4):
        cols = pl.multiple_of((((r + o) % 4) * 4 + g) * 1024, 1024)
        cp = pltpu.make_async_copy(sb_hbm.at[:, pl.ds(cols, 1024)], sb.at[o], sbsem.at[o])
        cp.start()
        csb.append(cp)
    cld = []
    for k in range(GROUPS):
        rows = pl.ds(k * 2048, 2048)
        cp = pltpu.make_async_copy(load_hbm.at[rows], ld.at[rows], insem.at[1, k])
        cp.start()
        cld.append(cp)

    cell = tcell_ref[...]
    chosen_xy = onehot((cell >> 7) == iota((64, 1024), 0))
    chosen_z = onehot((cell & 127) == iota((128, 1024), 0))
    mask = nt(chosen_xy, chosen_z).astype(BF)
    for k in range(4):
        m4[k * 64:(k + 1) * 64, :] = mask
    p, q = iota((256, 256), 0), iota((256, 256), 1)
    gg[...] = jnp.where((p >> 7) == (q >> 7), jnp.where(((p & 127) >> 3) == (q & 15), 1.0, 0.0), 0.0).astype(BF)
    ymask[...] = onehot((p & 7) == ((q & 127) >> 4))
    rmat[...] = onehot(iota((32, 256), 0) == (iota((32, 256), 1) >> 3))

    @pl.loop(0, 8)
    def _(k):
        rows = pl.ds(pl.multiple_of(k * 128, 128), 128)
        pbuf[rows, :] = onehot((cell >> 3) == iota((128, 1024), 0) + k * 128)

    for k in range(GROUPS):
        cin[k].wait()

        @pl.loop(k * UNITS // STEP, (k + 1) * UNITS // STEP)
        def _(i):
            for j in range(STEP):
                u = i * STEP + j
                a = v0[pl.ds(pl.multiple_of(u * 512, 512), 256), :] * m4[...]
                bb = v0[pl.ds(pl.multiple_of(u * 512 + 256, 256), 256), :] * m4[...]
                t = mm(jnp.concatenate([a, bb], axis=1), gg[...]).astype(BF) * ymask[...]
                t = mm(rmat[...], t)
                cbuf[pl.ds(pl.multiple_of(u * 64, 64), 32), :] = t[:, :128]
                cbuf[pl.ds(pl.multiple_of(u * 64 + 32, 32), 32), :] = t[:, 128:]

    for x in range(8):
        c2[:, x * 128:(x + 1) * 128] = cbuf[pl.ds(x, 128, stride=8), :].astype(BF)
    for h in range(2):
        tr[r, h] = mm(c2[...], pbuf[:, h * 512:(h + 1) * 512]).astype(BF)

    pl.semaphore_wait(barrier, peers)

    to_right = [rcopy(tr.at[r, h], tr.at[r, h], ts_s.at[0, h], ts_r.at[0, h], {"row": right}) for h in range(2)]
    to_left = [rcopy(tr.at[r, h], tr.at[r, h], ts_s.at[1, h], ts_r.at[1, h], {"row": left}) for h in range(2)]
    from_left = [rcopy(tr.at[left, h], tr.at[left, h], ts_s.at[0, h], ts_r.at[0, h], {"row": right}) for h in range(2)]
    from_right = [rcopy(tr.at[right, h], tr.at[right, h], ts_s.at[1, h], ts_r.at[1, h], {"row": left}) for h in range(2)]
    relay_right = rcopy(tr.at[left, 0], tr.at[left, 0], ts_s.at[2, 0], ts_r.at[2, 0], {"row": right})
    relay_left = rcopy(tr.at[right, 1], tr.at[right, 1], ts_s.at[2, 1], ts_r.at[2, 1], {"row": left})
    from_far = [
        rcopy(tr.at[far, 0], tr.at[far, 0], ts_s.at[2, 0], ts_r.at[2, 0], {"row": right}),
        rcopy(tr.at[far, 1], tr.at[far, 1], ts_s.at[2, 1], ts_r.at[2, 1], {"row": left}),
    ]
    to_right[0].start()
    to_left[1].start()
    to_right[1].start()
    to_left[0].start()

    p, q = iota((64, 128), 0), iota((64, 128), 1)
    d, o = p >> 4, p & 7
    qx, qy = (q >> 3) & 7, q & 7
    hit = jnp.where(
        d < 2,
        jnp.where(qx == d * 7, jnp.where(qy == o, 1.0, 0.0), 0.0),
        jnp.where(qy == (d - 2) * 7, jnp.where(qx == o, 1.0, 0.0), 0.0),
    )
    emat[...] = jnp.where(((p >> 3) & 1) == (q >> 6), hit, 0.0).astype(BF)
    p, q = iota((128, 256), 0), iota((128, 256), 1)
    px, py = (p >> 3) & 7, p & 7
    dx = jnp.abs(px - ((q >> 3) & 7))
    dy = jnp.abs(py - (q & 7))
    inside = jnp.where((p >> 6) == ((q >> 6) & 1), jnp.where(dx + dy == 1, 1.0, 0.0), 0.0)
    d, o = (q >> 4) & 7, q & 7
    hit = jnp.where(
        d < 2,
        jnp.where(px == d * 7, jnp.where(py == o, 1.0, 0.0), 0.0),
        jnp.where(py == (d - 2) * 7, jnp.where(px == o, 1.0, 0.0), 0.0),
    )
    hit = jnp.where(((q >> 3) & 1) == (p >> 6), hit, 0.0)
    ah[...] = jnp.where(q < 128, inside, hit)[:, :192].astype(BF)
    p, q = iota((256, 256), 0), iota((256, 256), 1)
    ss[...] = jnp.where((p >> 7) == (q >> 7), jnp.where(jnp.abs(p - q) == 1, 1.0, 0.0), 0.0).astype(BF)
    p, q = iota((16, 256), 0), iota((16, 256), 1)
    uu[...] = jnp.where(p < 4, jnp.where(q == (p >> 1) * 128 + (p & 1) * 127, 1.0, 0.0), 0.0).astype(BF)
    wz[...] = onehot(iota((16, 128), 1) == jnp.where(iota((16, 128), 0) < 2, iota((16, 128), 0) * 127, -1))

    w = OMEGA / (6.0 + coef_ref[...])
    for k in range(2):
        w4[k * 64:(k + 1) * 64, :] = w

    row8 = iota((8, 128), 0) & 3
    cells = jnp.zeros((8, 128), I32)
    weight = jnp.zeros((8, 128), F32)
    number = iota((64, 128), 0) * 128 + iota((64, 128), 1)
    for k in range(4):
        fc = fcell_ref[k]
        wk = jnp.sum(jnp.where(number == fc, w, 0.0), axis=(0, 1), keepdims=True)
        cells = jnp.where(row8 == k, fc, cells)
        weight = jnp.where(row8 == k, wk, weight)
    cinfo[...] = cells.astype(F32)
    for d in range(6):
        @pl.when(exists[d])
        def _(d=d):
            rcopy(cinfo, cnb.at[d ^ 1], i_s.at[d], i_r.at[d ^ 1], nbid[d]).start()

    for d in range(6):
        @pl.when(jnp.logical_not(exists[d]))
        def _(d=d):
            cnb[d] = jnp.zeros((8, 128), F32)
            gnb[d] = jnp.zeros((8, 128), F32)
            for s in range(3):
                if d < 4:
                    @pl.loop(0, 8)
                    def _(k, s=s):
                        hb[s, d, pl.ds(pl.multiple_of(k * 128, 128), 128), :] = jnp.zeros((128, 128), BF)
                else:
                    zh[s, d - 4] = jnp.zeros((NB, 256), F32)

    def halo(s, d, k):
        if d < 4:
            rows = pl.ds(pl.multiple_of(k * 256, 256), 256)
            src, dst = fs.at[s, d, rows], hb.at[s, d ^ 1, rows]
        else:
            rows = pl.ds(pl.multiple_of(k * 8, 8), 8)
            src, dst = zs.at[s, d - 4, rows], zh.at[s, (d ^ 1) - 4, rows]
        return rcopy(src, dst, hs_s.at[s, d, k], hs_r.at[s, d ^ 1, k], nbid[d])

    def send_halos(s, k):
        for d in (2, 3, 0, 1, 4, 5):
            @pl.when(exists[d])
            def _(d=d):
                halo(s, d, k).start()

    def wait_halos(s, k):
        for d in range(6):
            @pl.when(exists[d])
            def _(d=d):
                if d < 4:
                    rows = pl.ds(pl.multiple_of(k * 256, 256), 256)
                    dst = hb.at[s, d, rows]
                else:
                    rows = pl.ds(pl.multiple_of(k * 8, 8), 8)
                    dst = zh.at[s, d - 4, rows]
                rcopy(dst, dst, hs_s.at[s, d, k], hs_r.at[s, d, k], nbid[d]).wait_recv()

    def faces(s, u, pairs):
        for i, pair in enumerate(pairs):
            f = mm(emat[...], pair).astype(BF)
            for j in range(2):
                rows = pl.ds(pl.multiple_of(u * 64 + i * 32 + j * 16, 16), 16)
                for d in range(4):
                    fs[s, d, rows, :] = f[d * 16:(d + 1) * 16, j * 128:(j + 1) * 128]
            v = jnp.concatenate([pair[:, :128], pair[:, 128:]], axis=0)
            zf = nt(wz[...], v)
            for d in range(2):
                zs[s, d, pl.ds(2 * u + i, 1), :] = zf[d:d + 1, :]

    def sweep(s, u, vin, vout, more_rows, cols):
        v = [vin[pl.ds(pl.multiple_of(u * 512 + i * 128, 128), 128), :] for i in range(4)]
        rid = iota((16, 256), 0)
        ends = jnp.zeros((16, 256), F32)
        for i in range(2):
            for d in range(2):
                ends = jnp.where(rid == 2 * i + d, zh[s, d, pl.ds(2 * u + i, 1), :], ends)
        lhs = jnp.concatenate([ends] + more_rows, axis=0).astype(BF)
        t = tn(lhs, cols)
        wide = jnp.concatenate([jnp.concatenate(v[:2], axis=0), jnp.concatenate(v[2:], axis=0)], axis=1)
        z = mm(wide, ss[...]) + t
        pairs = []
        for i in range(2):
            sides = []
            for j in range(2):
                rows = pl.ds(pl.multiple_of(u * 64 + i * 32 + j * 16, 16), 16)
                sides.append(jnp.concatenate([v[2 * i + j]] + [hb[s, d, rows, :] for d in range(4)], axis=0))
            xy = mm(ah[...], jnp.concatenate(sides, axis=1))
            new = []
            for j in range(2):
                rows = pl.ds(pl.multiple_of(u * 512 + (2 * i + j) * 128, 128), 128)
                acc = xy[:, j * 128:(j + 1) * 128] + z[j * 128:(j + 1) * 128, i * 128:(i + 1) * 128]
                acc = acc + ld[rows, :].astype(F32)
                n = (0.2 * v[2 * i + j].astype(F32) + w4[...] * acc).astype(BF)
                vout[rows, :] = n
                new.append(n)
            pairs.append(jnp.concatenate(new, axis=1))
        return pairs

    def spread(u, values, places):
        pick = onehot(iota((128, 512), 0) == 8 * u + (iota((128, 512), 1) >> 6))
        m = mm(values, pick)
        return [m[:, :256] * places, m[:, 256:] * places]

    def sweep1(k):
        wait_halos(0, k)

        @pl.loop(k * UNITS // STEP, (k + 1) * UNITS // STEP)
        def _(i):
            for j in range(STEP):
                u = i * STEP + j
                faces(1, u, sweep(0, u, v0, v1, [], uu[...]))
        send_halos(1, k)

    for k in range(GROUPS):
        @pl.loop(k * UNITS // STEP, (k + 1) * UNITS // STEP)
        def _(i):
            for j in range(STEP):
                u = i * STEP + j
                v = [v0[pl.ds(pl.multiple_of(u * 512 + n * 128, 128), 128), :] for n in range(4)]
                faces(0, u, [jnp.concatenate(v[:2], axis=1), jnp.concatenate(v[2:], axis=1)])
        send_halos(0, k)
        if k == 1:
            from_left[0].wait_recv()
            relay_right.start()
            from_right[1].wait_recv()
            relay_left.start()

    for k in range(GROUPS):
        cld[k].wait()

    def product(o):
        csb[o].wait()
        src = (r + o) % 4
        return nt(sb[o, :, 0:512], tr[src, 0]) + nt(sb[o, :, 512:1024], tr[src, 1])

    part[...] = product(0)
    from_left[1].wait_recv()
    part[...] += product(3)
    from_right[0].wait_recv()
    part[...] += product(1)
    sweep1(0)
    from_far[0].wait_recv()
    from_far[1].wait_recv()
    total = (part[...] + product(2)).reshape(32, 8, 128)
    low, high = total[:, 0:4, :], total[:, 4:8, :]
    first = b == 0
    cown[...] = jnp.where(first, low, high)
    csend[...] = jnp.where(first, high, low)
    core = rcopy(csend, crecv, c_s, c_r, {"gz": g + 1 - 2 * b})
    core.start()
    sweep1(1)
    core.wait_recv()
    qbuf[...] = cown[...] + crecv[...]
    yrecv[y] = qbuf[pl.ds(y * 8, 8)]
    ycopies = []
    for o in range(1, 4):
        peer = (y + o) % 4
        cp = rcopy(qbuf.at[pl.ds(peer * 8, 8)], yrecv.at[y], y_s.at[o - 1], y_r.at[o - 1], {"col": peer * 4 + zl})
        cp.start()
        ycopies.append(cp)
    sweep1(2)
    for o in range(1, 4):
        peer = (y + 4 - o) % 4
        rcopy(yrecv.at[peer], yrecv.at[peer], y_s.at[o - 1], y_r.at[o - 1], {"col": peer * 4 + zl}).wait_recv()
    zsend[...] = (yrecv[0] + yrecv[1]) + (yrecv[2] + yrecv[3])
    zrecv[jz] = zsend[jz]
    zcopies = []
    for o in range(1, 8):
        peer = (jz + o) % 8
        cp = rcopy(zsend.at[peer], zrecv.at[jz], z_s.at[o - 1], z_r.at[o - 1], zdev(o))
        cp.start()
        zcopies.append(cp)
    sweep1(3)

    for d in range(6):
        @pl.when(exists[d])
        def _(d=d):
            rcopy(cnb.at[d], cnb.at[d], i_s.at[d], i_r.at[d], nbid[d]).wait_recv()
    mine = iota((8, 128), 0) < 4
    lane = iota((8, 256), 1) & 63
    for k in range(7):
        if k == 0:
            tx, ty, tz = cells >> 10, (cells >> 7) & 7, cells & 127
        else:
            ox, oy, oz = OFFS[k - 1]
            other = cnb[k - 1].astype(I32)
            at = jnp.where(mine, cells, other)
            tx = (at >> 10) + jnp.where(mine, ox, 7 * ox)
            ty = ((at >> 7) & 7) + jnp.where(mine, oy, 7 * oy)
            tz = (at & 127) + jnp.where(mine, oz, 127 * oz)
        txy = jnp.where((tx >= 0) & (tx < 8) & (ty >= 0) & (ty < 8), tx * 8 + ty, -1)
        tz = jnp.where((tz >= 0) & (tz < 128), tz, -1)
        spots = jnp.where(jnp.concatenate([txy, txy], axis=1) == lane, 1.0, 0.0)
        cols = jnp.where(tz == iota((8, 128), 1), 1.0, 0.0)
        lmask[k * 8:k * 8 + 8, :] = spots
        zcols[16 + k * 8:24 + k * 8, 0:128] = cols
        zcols[16 + k * 8:24 + k * 8, 128:256] = jnp.zeros((8, 128), F32)
        zcols[72 + k * 8:80 + k * 8, 0:128] = jnp.zeros((8, 128), F32)
        zcols[72 + k * 8:80 + k * 8, 128:256] = cols
        if k == 0:
            zcols3[16:24, 0:128] = cols
            zcols3[16:24, 128:256] = jnp.zeros((8, 128), F32)
            zcols3[24:32, 0:128] = jnp.zeros((8, 128), F32)
            zcols3[24:32, 128:256] = cols
    zcols[0:16, :] = uu[...].astype(F32)
    zcols3[0:16, :] = uu[...].astype(F32)

    for o in range(1, 8):
        peer = (jz + 8 - o) % 8
        rcopy(zrecv.at[peer], zrecv.at[peer], z_s.at[o - 1], z_r.at[o - 1], zdev(8 - o)).wait_recv()
    own = zrecv[0]
    for j in range(1, 8):
        own = own + zrecv[j]
    fbuf[...] = own
    own8 = jnp.concatenate([own, own], axis=0)
    gvals = weight * own8
    gbuf[...] = gvals
    for d in range(6):
        @pl.when(exists[d])
        def _(d=d):
            rcopy(gbuf, gnb.at[d ^ 1], g_s.at[d], g_r.at[d ^ 1], nbid[d]).start()
    fall[g] = own
    fcopies = []
    for o in range(1, 4):
        cp = rcopy(fbuf, fall.at[g], f_s.at[o - 1], f_r.at[o - 1], {"gz": (g + o) % 4})
        cp.start()
        fcopies.append(cp)

    for d in range(6):
        @pl.when(exists[d])
        def _(d=d):
            rcopy(gnb.at[d], gnb.at[d], g_s.at[d], g_r.at[d], nbid[d]).wait_recv()

    def split(values):
        hi = values.astype(BF).astype(F32)
        return hi, values - hi

    hi, lo = split(1.2 * own8)
    val[0:8, :] = jnp.where(mine, hi, lo)
    for d in range(6):
        val[8 + d * 8:16 + d * 8, :] = jnp.where(mine, gvals, gnb[d])
    hi, lo = split(own8)
    val3[...] = jnp.where(mine, hi, lo)

    @pl.loop(0, GROUPS)
    def _(k):
        wait_halos(1, k)

        @pl.loop(k * UNITS // STEP, (k + 1) * UNITS // STEP)
        def _(i):
            for j in range(STEP):
                u = i * STEP + j
                rows = spread(u, val[...].astype(BF), lmask[...])
                faces(2, u, sweep(1, u, v1, v2, rows, zcols[...].astype(BF)))
        send_halos(2, k)

    def put(k):
        rows = pl.ds(pl.multiple_of(k * 2048, 2048), 2048)
        return pltpu.make_async_copy(v3.at[rows], out_hbm.at[rows], outsem.at[k])

    @pl.loop(0, GROUPS)
    def _(k):
        wait_halos(2, k)

        @pl.loop(k * UNITS // STEP, (k + 1) * UNITS // STEP)
        def _(i):
            for j in range(STEP):
                u = i * STEP + j
                rows = spread(u, val3[...].astype(BF), lmask[0:8, :])
                sweep(2, u, v2, v3, rows, zcols3[...].astype(BF))
        put(k).start()

    for o in range(1, 4):
        peer = (g + 4 - o) % 4
        rcopy(fall.at[peer], fall.at[peer], f_s.at[o - 1], f_r.at[o - 1], {"gz": peer}).wait_recv()
    sel = jnp.where(iota((32, 128), 1) == g * 32 + iota((32, 128), 0), 1.0, 0.0)
    rows16 = jnp.concatenate([fall[0], fall[1], fall[2], fall[3]], axis=0)
    flux_ref[...] = nt(sel, rows16, precision=lax.Precision.HIGHEST)

    for cp in to_right + to_left + [relay_right, relay_left, core] + ycopies + zcopies + fcopies:
        cp.wait_send()
    for d in range(6):
        @pl.when(exists[d])
        def _(d=d):
            rcopy(cinfo, cnb.at[d ^ 1], i_s.at[d], i_r.at[d ^ 1], nbid[d]).wait_send()
            rcopy(gbuf, gnb.at[d ^ 1], g_s.at[d], g_r.at[d ^ 1], nbid[d]).wait_send()
            for s in range(3):
                @pl.loop(0, GROUPS)
                def _(k):
                    halo(s, d, k).wait_send()
    for k in range(GROUPS):
        put(k).wait()


def per_device(volume_field, volume_load, coefficient, surface_block, trace_cell, flux_cell):
    side_count, first_span, second_span, third_span = volume_field.shape
    rows = side_count * first_span * second_span
    vm = pltpu.VMEM
    dma = pltpu.SemaphoreType.DMA
    scratch = [
        vm((rows, 128), BF), vm((rows, 128), BF), vm((rows, 128), BF), vm((rows, 128), BF), vm((rows, 128), BF),
        vm((4, 256, 1024), BF), vm((4, 2, 128, 512), BF), vm((128, 128), F32),
        vm((3, 4, 1024, 128), BF), vm((3, 4, 1024, 128), BF), vm((3, 2, NB, 256), F32), vm((3, 2, NB, 256), F32),
        vm((128, 192), BF), vm((64, 128), BF), vm((256, 256), BF), vm((256, 256), BF),
        vm((32, 256), BF), vm((16, 128), BF), vm((16, 256), BF), vm((256, 128), BF), vm((256, 256), BF),
        vm((1024, 128), F32), vm((128, 1024), BF),
        vm((1024, 1024), BF),
        vm((256, 128), F32), vm((32, 4, 128), F32), vm((32, 4, 128), F32), vm((32, 4, 128), F32),
        vm((32, 4, 128), F32), vm((4, 8, 4, 128), F32), vm((8, 4, 128), F32), vm((8, 4, 128), F32),
        vm((4, 128), F32), vm((4, 4, 128), F32),
        vm((8, 128), F32), vm((6, 8, 128), F32), vm((8, 128), F32), vm((6, 8, 128), F32),
        vm((56, 256), F32), vm((128, 256), F32), vm((32, 256), F32), vm((56, 128), F32), vm((8, 128), F32),
        dma((2, GROUPS)), dma((4,)), dma((GROUPS,)), dma((3, 6, GROUPS)), dma((3, 6, GROUPS)),
        dma((3, 2)), dma((3, 2)), dma, dma, dma((3,)), dma((3,)), dma((7,)), dma((7,)),
        dma((3,)), dma((3,)), dma((6,)), dma((6,)), dma((6,)), dma((6,)),
    ]
    anywhere = pl.BlockSpec(memory_space=pl.ANY)
    local = pl.BlockSpec(memory_space=pltpu.VMEM)
    new_field, surface_flux = pl.pallas_call(
        kernel,
        out_shape=(jax.ShapeDtypeStruct((rows, 128), BF), jax.ShapeDtypeStruct((32, 16), F32)),
        in_specs=[anywhere, anywhere, local, anywhere, local, pl.BlockSpec(memory_space=pltpu.SMEM)],
        out_specs=(anywhere, local),
        scratch_shapes=scratch,
        compiler_params=pltpu.CompilerParams(
            collective_id=0, has_side_effects=True, vmem_limit_bytes=60 * 1024 * 1024
        ),
    )(
        volume_field.reshape(rows, 128),
        volume_load.reshape(rows, 128),
        coefficient.reshape(64, 128),
        surface_block,
        trace_cell.reshape(1, 1024),
        flux_cell.reshape(4),
    )
    return new_field.reshape(volume_field.shape), surface_flux


def solution(mesh):
    in_specs = (
        P(None, "row", "col", "gz"),
        P(None, "row", "col", "gz"),
        P("row", "col", "gz"),
        P("row", "col"),
        P("row", "col", "gz", None),
        P("row", "col", "gz", None),
    )
    out_specs = (P(None, "row", "col", "gz"), P("gz", ("row", "col")))
    return jax.shard_map(
        per_device, mesh=mesh, in_specs=in_specs, out_specs=out_specs, check_vma=False
    )
```

```python
import functools

import jax
import jax.numpy as jnp
from jax import lax
from jax.experimental import pallas as pl
from jax.experimental.pallas import tpu as pltpu
from jax.sharding import PartitionSpec as P

MESH = pl.DeviceIdType.MESH
BF = jnp.bfloat16
F32 = jnp.float32
I32 = jnp.int32
OMEGA = 0.8
GROUPS = 4
STEPS = 2
NB = GROUPS * STEPS * 4
OFFS = ((-1, 0, 0), (1, 0, 0), (0, -1, 0), (0, 1, 0), (0, 0, -1), (0, 0, 1))


def iota(shape, dim):
    return lax.broadcasted_iota(I32, shape, dim)


def onehot(cond):
    return jnp.where(cond, 1.0, 0.0).astype(BF)


def nt(a, b, **kw):
    return lax.dot_general(a, b, (((1,), (1,)), ((), ())), preferred_element_type=F32, **kw)


def tn(a, b):
    return lax.dot_general(a, b, (((0,), (0,)), ((), ())), preferred_element_type=F32)


def mm(a, b):
    return jnp.dot(a, b, preferred_element_type=F32)


def kernel(
    field_hbm, load_hbm, coef_ref, sb_hbm, tcell_ref, fcell_ref,
    out_hbm, flux_ref,
    v0, ld, v1, v2, v3, sb, tr, w4, hb, fs, zh, zs,
    ah, emat, ss, gg, rmat, wz, uu, m4, ymask, cbuf, c2, pbuf, xall,
    part, cown, csend, crecv, qbuf, yrecv, zsend, zrecv, fbuf, fall,
    gbuf, gnb, cinfo, cnb, lmask, zcols, zcols3, val, val3,
    insem, ldsem, sbsem, outsem, hs_s, hs_r, ts_s, ts_r, c_s, c_r, y_s, y_r, z_s, z_r,
    f_s, f_r, g_s, g_r, i_s, i_r,
):
    r = lax.axis_index("row")
    c = lax.axis_index("col")
    g = lax.axis_index("gz")
    y, zl = c // 4, c % 4
    zhi, b = g // 2, g % 2
    right, left, far = (r + 1) % 4, (r + 3) % 4, (r + 2) % 4
    jz = zl * 2 + zhi

    exists = (r > 0, r < 3, c > 0, c < 15, g > 0, g < 3)
    nbid = ({"row": r - 1}, {"row": r + 1}, {"col": c - 1}, {"col": c + 1}, {"gz": g - 1}, {"gz": g + 1})

    def rcopy(src, dst, ss, rs, dev):
        return pltpu.make_async_remote_copy(
            src_ref=src, dst_ref=dst, send_sem=ss, recv_sem=rs, device_id=dev, device_id_type=MESH
        )

    barrier = pltpu.get_barrier_semaphore()

    def greet(dev):
        pl.semaphore_signal(barrier, inc=1, device_id=dev, device_id_type=MESH)

    def zdev(o):
        j = (jz + o) % 8
        return {"col": y * 4 + j // 2, "gz": (j % 2) * 2 + b}

    for o in range(1, 4):
        greet({"row": (r + o) % 4})
        greet({"col": ((y + o) % 4) * 4 + zl})
    for o in range(1, 8):
        greet(zdev(o))
    greet({"gz": zhi * 2 + 1 - b})
    greet({"gz": (1 - zhi) * 2 + 1 - b})
    wraps = ((zl == 0) & (c > 0), (zl == 3) & (c < 15))
    for d in range(2):
        @pl.when(wraps[d])
        def _(d=d):
            greet(nbid[2 + d])
    peers = 15 + jnp.where(wraps[0], 1, 0) + jnp.where(wraps[1], 1, 0)

    cin = []
    for k in range(GROUPS):
        rows = pl.ds(k * 2048, 2048)
        cp = pltpu.make_async_copy(field_hbm.at[rows], v0.at[rows], insem.at[k])
        cp.start()
        cin.append(cp)
    for o in range(4):
        cols = pl.multiple_of((((r + o) % 4) * 4 + g) * 1024, 1024)
        pltpu.make_async_copy(sb_hbm.at[:, pl.ds(cols, 1024)], sb.at[o], sbsem).start()
    cld = pltpu.make_async_copy(load_hbm, ld, ldsem)
    cld.start()

    cell = tcell_ref[...]
    chosen_xy = onehot((cell >> 7) == iota((64, 1024), 0))
    chosen_z = onehot((cell & 127) == iota((128, 1024), 0))
    mask = nt(chosen_xy, chosen_z).astype(BF)
    for k in range(4):
        m4[k * 64:(k + 1) * 64, :] = mask
    p, q = iota((256, 256), 0), iota((256, 256), 1)
    gg[...] = jnp.where((p >> 7) == (q >> 7), jnp.where(((p & 127) >> 3) == (q & 15), 1.0, 0.0), 0.0).astype(BF)
    ymask[...] = onehot((p & 7) == ((q & 127) >> 4))
    rmat[...] = onehot(iota((32, 256), 0) == (iota((32, 256), 1) >> 3))

    @pl.loop(0, 8)
    def _(k):
        rows = pl.ds(pl.multiple_of(k * 128, 128), 128)
        pbuf[rows, :] = onehot((cell >> 3) == iota((128, 1024), 0) + k * 128)

    for k in range(GROUPS):
        cin[k].wait()

        @pl.loop(k * STEPS, (k + 1) * STEPS)
        def _(i):
            a = [v0[pl.ds(pl.multiple_of(i * 1024 + n * 256, 256), 256), :] * m4[...] for n in range(4)]
            a = [jnp.concatenate(a[:2], axis=1), jnp.concatenate(a[2:], axis=1)]
            t = mm(jnp.concatenate(a, axis=0), gg[...]).astype(BF)
            for n in range(2):
                c = mm(rmat[...], t[n * 256:(n + 1) * 256, :] * ymask[...])
                cbuf[pl.ds(pl.multiple_of(i * 128 + n * 64, 64), 32), :] = c[:, :128]
                cbuf[pl.ds(pl.multiple_of(i * 128 + n * 64 + 32, 32), 32), :] = c[:, 128:]

    for x in range(8):
        c2[:, x * 128:(x + 1) * 128] = cbuf[pl.ds(x, 128, stride=8), :].astype(BF)
    for h in range(2):
        tr[r, h] = mm(c2[...], pbuf[:, h * 512:(h + 1) * 512]).astype(BF)

    pl.semaphore_wait(barrier, peers)

    def half(who, h, sem, dev):
        return rcopy(tr.at[who, h], tr.at[who, h], ts_s, ts_r.at[sem], {"row": dev})

    to_right = [half(r, 0, 0, right), half(r, 1, 2, right)]
    to_left = [half(r, 0, 2, left), half(r, 1, 1, left)]
    from_left = half(left, 0, 0, right)
    from_right = half(right, 1, 1, left)
    relay_right = half(left, 0, 3, right)
    relay_left = half(right, 1, 3, left)
    from_sides = rcopy(tr.at[far], tr.at[far], ts_s, ts_r.at[2], {"row": right})
    from_far = rcopy(tr.at[far], tr.at[far], ts_s, ts_r.at[3], {"row": right})
    to_right[0].start()
    to_left[1].start()
    to_right[1].start()
    to_left[0].start()

    p, q = iota((64, 128), 0), iota((64, 128), 1)
    d, o = p >> 4, p & 7
    qx, qy = (q >> 3) & 7, q & 7
    hit = jnp.where(
        d < 2,
        jnp.where(qx == d * 7, jnp.where(qy == o, 1.0, 0.0), 0.0),
        jnp.where(qy == (d - 2) * 7, jnp.where(qx == o, 1.0, 0.0), 0.0),
    )
    emat[...] = jnp.where(((p >> 3) & 1) == (q >> 6), hit, 0.0).astype(BF)
    p, q = iota((128, 256), 0), iota((128, 256), 1)
    px, py = (p >> 3) & 7, p & 7
    dx = jnp.abs(px - ((q >> 3) & 7))
    dy = jnp.abs(py - (q & 7))
    inside = jnp.where((p >> 6) == ((q >> 6) & 1), jnp.where(dx + dy == 1, 1.0, 0.0), 0.0)
    d, o = (q >> 4) & 7, q & 7
    hit = jnp.where(
        d < 2,
        jnp.where(px == d * 7, jnp.where(py == o, 1.0, 0.0), 0.0),
        jnp.where(py == (d - 2) * 7, jnp.where(px == o, 1.0, 0.0), 0.0),
    )
    hit = jnp.where(((q >> 3) & 1) == (p >> 6), hit, 0.0)
    ah[...] = jnp.where(q < 128, inside, hit)[:, :192].astype(BF)
    p, q = iota((256, 256), 0), iota((256, 256), 1)
    ss[...] = jnp.where((p >> 7) == (q >> 7), jnp.where(jnp.abs(p - q) == 1, 1.0, 0.0), 0.0).astype(BF)
    p, q = iota((16, 256), 0), iota((16, 256), 1)
    uu[...] = jnp.where(p < 4, jnp.where(q == (p >> 1) * 128 + (p & 1) * 127, 1.0, 0.0), 0.0).astype(BF)
    wz[...] = onehot(iota((16, 128), 1) == jnp.where(iota((16, 128), 0) < 2, iota((16, 128), 0) * 127, -1))

    w = OMEGA / (6.0 + coef_ref[...])
    for k in range(2):
        w4[k * 64:(k + 1) * 64, :] = w

    row8 = iota((8, 128), 0) & 3
    cells = jnp.zeros((8, 128), I32)
    weight = jnp.zeros((8, 128), F32)
    number = iota((64, 128), 0) * 128 + iota((64, 128), 1)
    for k in range(4):
        fc = fcell_ref[k]
        wk = jnp.sum(jnp.where(number == fc, w, 0.0), axis=(0, 1), keepdims=True)
        cells = jnp.where(row8 == k, fc, cells)
        weight = jnp.where(row8 == k, wk, weight)
    cinfo[...] = cells.astype(F32)
    for d in range(6):
        @pl.when(exists[d])
        def _(d=d):
            rcopy(cinfo, cnb.at[d ^ 1], i_s.at[d], i_r.at[d ^ 1], nbid[d]).start()

    for d in range(6):
        @pl.when(jnp.logical_not(exists[d]))
        def _(d=d):
            cnb[d] = jnp.zeros((8, 128), F32)
            gnb[d] = jnp.zeros((8, 128), F32)
            for s in range(3):
                if d < 4:
                    @pl.loop(0, 8)
                    def _(k, s=s):
                        hb[s, d, pl.ds(pl.multiple_of(k * 128, 128), 128), :] = jnp.zeros((128, 128), BF)
                else:
                    zh[s, d - 4] = jnp.zeros((NB, 256), F32)

    def halo(s, d, k):
        if d < 4:
            rows = pl.ds(pl.multiple_of(k * 256, 256), 256)
            src, dst = fs.at[s, d, rows], hb.at[s, d ^ 1, rows]
        else:
            rows = pl.ds(pl.multiple_of(k * 8, 8), 8)
            src, dst = zs.at[s, d - 4, rows], zh.at[s, (d ^ 1) - 4, rows]
        return rcopy(src, dst, hs_s.at[d], hs_r.at[s % 2, d ^ 1, k], nbid[d])

    def send_halos(s, k, dirs=(2, 3, 0, 1, 4, 5)):
        for d in dirs:
            @pl.when(exists[d])
            def _(d=d):
                halo(s, d, k).start()

    def wait_halos(s, k):
        for d in range(6):
            @pl.when(exists[d])
            def _(d=d):
                if d < 4:
                    rows = pl.ds(pl.multiple_of(k * 256, 256), 256)
                    dst = hb.at[s, d, rows]
                else:
                    rows = pl.ds(pl.multiple_of(k * 8, 8), 8)
                    dst = zh.at[s, d - 4, rows]
                rcopy(dst, dst, hs_s.at[d], hs_r.at[s % 2, d, k], nbid[d]).wait_recv()

    def faces(s, i, pairs):
        for n, pair in enumerate(pairs):
            f = mm(emat[...], pair).astype(BF)
            for j in range(2):
                rows = pl.ds(pl.multiple_of(i * 128 + n * 32 + j * 16, 16), 16)
                for d in range(4):
                    fs[s, d, rows, :] = f[d * 16:(d + 1) * 16, j * 128:(j + 1) * 128]
            v = jnp.concatenate([pair[:, :128], pair[:, 128:]], axis=0)
            zf = nt(wz[...], v)
            for d in range(2):
                zs[s, d, pl.ds(4 * i + n, 1), :] = zf[d:d + 1, :]

    def sweep(s, i, vin, vout, more_rows, cols):
        v = [vin[pl.ds(pl.multiple_of(i * 1024 + n * 128, 128), 128), :] for n in range(8)]
        rid = iota((16, 256), 0)
        lhs = []
        for n in range(2):
            ends = jnp.zeros((16, 256), F32)
            for j in range(2):
                for d in range(2):
                    ends = jnp.where(rid == 2 * j + d, zh[s, d, pl.ds(4 * i + 2 * n + j, 1), :], ends)
            lhs.append(ends)
        lhs = jnp.concatenate([jnp.concatenate(lhs, axis=1)] + more_rows, axis=0).astype(BF)
        t = tn(lhs, cols)
        wide = [
            jnp.concatenate([jnp.concatenate(v[n:n + 2], axis=0), jnp.concatenate(v[n + 2:n + 4], axis=0)], axis=1)
            for n in (0, 4)
        ]
        z = mm(jnp.concatenate(wide, axis=0), ss[...]) + t
        pairs = []
        for n in range(4):
            sides = []
            for j in range(2):
                rows = pl.ds(pl.multiple_of(i * 128 + n * 32 + j * 16, 16), 16)
                sides.append(jnp.concatenate([v[2 * n + j]] + [hb[s, d, rows, :] for d in range(4)], axis=0))
            xy = mm(ah[...], jnp.concatenate(sides, axis=1))
            new = []
            for j in range(2):
                rows = pl.ds(pl.multiple_of(i * 1024 + (2 * n + j) * 128, 128), 128)
                top = (n // 2) * 256 + j * 128
                acc = xy[:, j * 128:(j + 1) * 128] + z[top:top + 128, (n % 2) * 128:(n % 2 + 1) * 128]
                acc = acc + ld[rows, :].astype(F32)
                fresh = (0.2 * v[2 * n + j].astype(F32) + w4[...] * acc).astype(BF)
                vout[rows, :] = fresh
                new.append(fresh)
            pairs.append(jnp.concatenate(new, axis=1))
        return pairs

    def spread(i, values, places):
        m = mm(values, xall[:, pl.ds(pl.multiple_of(i * 1024, 1024), 1024)])
        m = [m[:, n * 256:(n + 1) * 256] * places for n in range(4)]
        return [jnp.concatenate([m[0], m[2]], axis=1), jnp.concatenate([m[1], m[3]], axis=1)]

    def sweep1(k):
        wait_halos(0, k)

        @pl.loop(k * STEPS, (k + 1) * STEPS)
        def _(i):
            faces(1, i, sweep(0, i, v0, v1, [], uu[...]))

    for k in range(GROUPS):
        @pl.loop(k * STEPS, (k + 1) * STEPS)
        def _(i):
            v = [v0[pl.ds(pl.multiple_of(i * 1024 + n * 128, 128), 128), :] for n in range(8)]
            faces(0, i, [jnp.concatenate(v[2 * n:2 * n + 2], axis=1) for n in range(4)])
        send_halos(0, k, (2, 3, 4, 5))
    from_left.wait_recv()
    relay_right.start()
    from_right.wait_recv()
    relay_left.start()
    for k in range(GROUPS):
        send_halos(0, k, (0, 1))
    cld.wait()
    pltpu.make_async_copy(sb, sb, sbsem).wait()

    def product(o):
        src = (r + o) % 4
        return nt(sb[o, :, 0:512], tr[src, 0]) + nt(sb[o, :, 512:1024], tr[src, 1])

    part[...] = product(0)
    from_sides.wait_recv()
    part[...] += product(3)
    part[...] += product(1)
    from_far.wait_recv()
    total = (part[...] + product(2)).reshape(32, 8, 128)
    low, high = total[:, 0:4, :], total[:, 4:8, :]
    first = b == 0
    cown[...] = jnp.where(first, low, high)
    csend[...] = jnp.where(first, high, low)
    core = rcopy(csend, crecv, c_s, c_r, {"gz": g + 1 - 2 * b})
    core.start()

    @pl.loop(0, 8)
    def _(k):
        at = k * 1024 + iota((128, 1024), 1)
        xall[:, pl.ds(pl.multiple_of(k * 1024, 1024), 1024)] = onehot(iota((128, 1024), 0) == (at >> 6))

    core.wait_recv()
    qbuf[...] = cown[...] + crecv[...]
    yrecv[y] = qbuf[pl.ds(y * 8, 8)]
    for o in range(1, 4):
        peer = (y + o) % 4
        cp = rcopy(qbuf.at[pl.ds(peer * 8, 8)], yrecv.at[y], y_s, y_r, {"col": peer * 4 + zl})
        cp.start()
    sweep1(0)
    send_halos(1, 0)
    three = pl.ds(0, 24)
    yall = rcopy(qbuf.at[three], qbuf.at[three], y_s, y_r, {"col": ((y + 1) % 4) * 4 + zl})
    yall.wait_recv()
    zsend[...] = (yrecv[0] + yrecv[1]) + (yrecv[2] + yrecv[3])
    zrecv[jz] = zsend[jz]
    for o in range(1, 8):
        peer = (jz + o) % 8
        cp = rcopy(zsend.at[peer], zrecv.at[jz], z_s, z_r, zdev(o))
        cp.start()
    sweep1(1)
    send_halos(1, 1)

    for d in range(6):
        @pl.when(exists[d])
        def _(d=d):
            rcopy(cnb.at[d], cnb.at[d], i_s.at[d], i_r.at[d], nbid[d]).wait_recv()
    mine = iota((8, 128), 0) < 4
    lane = iota((8, 256), 1) & 63
    for k in range(7):
        if k == 0:
            tx, ty, tz = cells >> 10, (cells >> 7) & 7, cells & 127
        else:
            ox, oy, oz = OFFS[k - 1]
            other = cnb[k - 1].astype(I32)
            at = jnp.where(mine, cells, other)
            tx = (at >> 10) + jnp.where(mine, ox, 7 * ox)
            ty = ((at >> 7) & 7) + jnp.where(mine, oy, 7 * oy)
            tz = (at & 127) + jnp.where(mine, oz, 127 * oz)
        txy = jnp.where((tx >= 0) & (tx < 8) & (ty >= 0) & (ty < 8), tx * 8 + ty, -1)
        tz = jnp.where((tz >= 0) & (tz < 128), tz, -1)
        spots = jnp.where(jnp.concatenate([txy, txy], axis=1) == lane, 1.0, 0.0)
        cols = jnp.where(tz == iota((8, 128), 1), 1.0, 0.0)
        lmask[k * 8:k * 8 + 8, :] = spots
        zcols[16 + k * 8:24 + k * 8, 0:128] = cols
        zcols[16 + k * 8:24 + k * 8, 128:256] = jnp.zeros((8, 128), F32)
        zcols[72 + k * 8:80 + k * 8, 0:128] = jnp.zeros((8, 128), F32)
        zcols[72 + k * 8:80 + k * 8, 128:256] = cols
        if k == 0:
            zcols3[16:24, 0:128] = cols
            zcols3[16:24, 128:256] = jnp.zeros((8, 128), F32)
            zcols3[24:32, 0:128] = jnp.zeros((8, 128), F32)
            zcols3[24:32, 128:256] = cols
    zcols[0:16, :] = uu[...].astype(F32)
    zcols3[0:16, :] = uu[...].astype(F32)

    sweep1(2)
    seven = pl.ds(0, 7)
    zall = rcopy(zsend.at[seven], zrecv.at[seven], z_s, z_r, zdev(1))
    zall.wait_recv()
    own = zrecv[0]
    for j in range(1, 8):
        own = own + zrecv[j]
    fbuf[...] = own
    own8 = jnp.concatenate([own, own], axis=0)
    gvals = weight * own8
    gbuf[...] = gvals
    for d in range(6):
        @pl.when(exists[d])
        def _(d=d):
            rcopy(gbuf, gnb.at[d ^ 1], g_s.at[d], g_r.at[d ^ 1], nbid[d]).start()
    fall[g] = own
    for o in range(1, 4):
        cp = rcopy(fbuf, fall.at[g], f_s, f_r, {"gz": (g + o) % 4})
        cp.start()
    send_halos(1, 2)
    sweep1(3)
    send_halos(1, 3)

    for d in range(6):
        @pl.when(exists[d])
        def _(d=d):
            rcopy(gnb.at[d], gnb.at[d], g_s.at[d], g_r.at[d], nbid[d]).wait_recv()

    def split(values):
        hi = values.astype(BF).astype(F32)
        return hi, values - hi

    hi, lo = split(1.2 * own8)
    val[0:8, :] = jnp.where(mine, hi, lo)
    for d in range(6):
        val[8 + d * 8:16 + d * 8, :] = jnp.where(mine, gvals, gnb[d])
    hi, lo = split(own8)
    val3[...] = jnp.where(mine, hi, lo)

    @pl.loop(0, GROUPS)
    def _(k):
        wait_halos(1, k)

        @pl.loop(k * STEPS, (k + 1) * STEPS)
        def _(i):
            rows = spread(i, val[...].astype(BF), lmask[...])
            faces(2, i, sweep(1, i, v1, v2, rows, zcols[...].astype(BF)))
        send_halos(2, k)

    def put(k):
        rows = pl.ds(pl.multiple_of(k * 2048, 2048), 2048)
        return pltpu.make_async_copy(v3.at[rows], out_hbm.at[rows], outsem)

    @pl.loop(0, GROUPS)
    def _(k):
        wait_halos(2, k)

        @pl.loop(k * STEPS, (k + 1) * STEPS)
        def _(i):
            rows = spread(i, val3[...].astype(BF), lmask[0:8, :])
            sweep(2, i, v2, v3, rows, zcols3[...].astype(BF))
        put(k).start()

    others = pl.ds(0, 3)
    fgot = rcopy(zsend.at[others], fall.at[others], f_s, f_r, {"gz": (g + 1) % 4})
    fgot.wait_recv()
    sel = jnp.where(iota((32, 128), 1) == g * 32 + iota((32, 128), 0), 1.0, 0.0)
    rows16 = jnp.concatenate([fall[0], fall[1], fall[2], fall[3]], axis=0)
    flux_ref[...] = nt(rows16, sel, precision=lax.Precision.HIGHEST)

    sent = pl.ds(0, 3)
    rcopy(tr.at[sent], tr.at[sent], ts_s, ts_r.at[0], {"row": right}).wait_send()
    for cp in (core, yall, zall, fgot):
        cp.wait_send()
    for d in range(6):
        @pl.when(exists[d])
        def _(d=d):
            rcopy(cinfo, cnb.at[d ^ 1], i_s.at[d], i_r.at[d ^ 1], nbid[d]).wait_send()
            rcopy(gbuf, gnb.at[d ^ 1], g_s.at[d], g_r.at[d ^ 1], nbid[d]).wait_send()
            sent = fs.at[:, d] if d < 4 else zs.at[:, d - 4]
            rcopy(sent, sent, hs_s.at[d], hs_r.at[0, d, 0], nbid[d]).wait_send()
    pltpu.make_async_copy(v3, out_hbm, outsem).wait()


def per_device(volume_field, volume_load, coefficient, surface_block, trace_cell, flux_cell):
    side_count, first_span, second_span, third_span = volume_field.shape
    rows = side_count * first_span * second_span
    vm = pltpu.VMEM
    dma = pltpu.SemaphoreType.DMA
    scratch = [
        vm((rows, 128), BF), vm((rows, 128), BF), vm((rows, 128), BF), vm((rows, 128), BF), vm((rows, 128), BF),
        vm((4, 256, 1024), BF), vm((4, 2, 128, 512), BF), vm((128, 128), F32),
        vm((3, 4, 1024, 128), BF), vm((3, 4, 1024, 128), BF), vm((3, 2, NB, 256), F32), vm((3, 2, NB, 256), F32),
        vm((128, 192), BF), vm((64, 128), BF), vm((256, 256), BF), vm((256, 256), BF),
        vm((32, 256), BF), vm((16, 128), BF), vm((16, 256), BF), vm((256, 128), BF), vm((256, 256), BF),
        vm((1024, 128), F32), vm((128, 1024), BF),
        vm((1024, 1024), BF), vm((128, 8192), BF),
        vm((256, 128), F32), vm((32, 4, 128), F32), vm((32, 4, 128), F32), vm((32, 4, 128), F32),
        vm((32, 4, 128), F32), vm((4, 8, 4, 128), F32), vm((8, 4, 128), F32), vm((8, 4, 128), F32),
        vm((4, 128), F32), vm((4, 4, 128), F32),
        vm((8, 128), F32), vm((6, 8, 128), F32), vm((8, 128), F32), vm((6, 8, 128), F32),
        vm((56, 256), F32), vm((128, 256), F32), vm((32, 256), F32), vm((56, 128), F32), vm((8, 128), F32),
        dma((GROUPS,)), dma, dma, dma, dma((6,)), dma((2, 6, GROUPS)),
        dma, dma((4,)), dma, dma, dma, dma, dma, dma, dma, dma, dma((6,)), dma((6,)), dma((6,)), dma((6,)),
    ]
    anywhere = pl.BlockSpec(memory_space=pl.ANY)
    local = pl.BlockSpec(memory_space=pltpu.VMEM)
    new_field, surface_flux = pl.pallas_call(
        kernel,
        out_shape=(jax.ShapeDtypeStruct((rows, 128), BF), jax.ShapeDtypeStruct((16, 32), F32)),
        in_specs=[anywhere, anywhere, local, anywhere, local, pl.BlockSpec(memory_space=pltpu.SMEM)],
        out_specs=(anywhere, local),
        scratch_shapes=scratch,
        compiler_params=pltpu.CompilerParams(
            collective_id=0, has_side_effects=True, vmem_limit_bytes=60 * 1024 * 1024
        ),
    )(
        volume_field.reshape(rows, 128),
        volume_load.reshape(rows, 128),
        coefficient.reshape(64, 128),
        surface_block,
        trace_cell.reshape(1, 1024),
        flux_cell.reshape(4),
    )
    return new_field.reshape(volume_field.shape), surface_flux.T


def solution(mesh):
    in_specs = (
        P(None, "row", "col", "gz"),
        P(None, "row", "col", "gz"),
        P("row", "col", "gz"),
        P("row", "col"),
        P("row", "col", "gz", None),
        P("row", "col", "gz", None),
    )
    out_specs = (P(None, "row", "col", "gz"), P("gz", ("row", "col")))
    return jax.shard_map(
        per_device, mesh=mesh, in_specs=in_specs, out_specs=out_specs, check_vma=False
    )
```

```python
import functools

import jax
import jax.numpy as jnp
from jax import lax
from jax.experimental import pallas as pl
from jax.experimental.pallas import tpu as pltpu
from jax.sharding import PartitionSpec as P

MESH = pl.DeviceIdType.MESH
BF = jnp.bfloat16
F32 = jnp.float32
I32 = jnp.int32
OMEGA = 0.8
GROUPS = 8
OFFS = ((-1, 0, 0), (1, 0, 0), (0, -1, 0), (0, 1, 0), (0, 0, -1), (0, 0, 1))


def iota(shape, dim):
    return lax.broadcasted_iota(I32, shape, dim)


def onehot(cond):
    return jnp.where(cond, 1.0, 0.0).astype(BF)


def nt(a, b, **kw):
    return lax.dot_general(a, b, (((1,), (1,)), ((), ())), preferred_element_type=F32, **kw)


def tn(a, b):
    return lax.dot_general(a, b, (((0,), (0,)), ((), ())), preferred_element_type=F32)


def mm(a, b):
    return jnp.dot(a, b, preferred_element_type=F32)


def kernel(
    field_hbm, load_hbm, coef_ref, sb_hbm, tcell_ref, fcell_ref,
    out_hbm, flux_ref,
    v0, ld, v1, v2, v3, sb, tr, w4, hb, fs, zh, zs,
    ah, emat, ss, gg, wz, uu, m4, picked, cbuf, c2, pbuf, xall,
    part, cown, csend, crecv, qbuf, zrecv, fbuf, fall,
    gbuf, gnb, cinfo, cnb, lmask, zcols, zcols3, val, val3,
    insem, ldsem, sbsem, outsem, hs_s, hs_r, ts_s, ts_r, c_s, c_r, z_s, z_r, round_sem,
    f_s, f_r, g_s, g_r, i_s, i_r,
):
    r = lax.axis_index("row")
    c = lax.axis_index("col")
    g = lax.axis_index("gz")
    y, zl = c // 4, c % 4
    zhi, b = g // 2, g % 2
    right, left, far = (r + 1) % 4, (r + 3) % 4, (r + 2) % 4
    me = c * 2 + zhi

    exists = (r > 0, r < 3, c > 0, c < 15, g > 0, g < 3)
    nbid = ({"row": r - 1}, {"row": r + 1}, {"col": c - 1}, {"col": c + 1}, {"gz": g - 1}, {"gz": g + 1})

    def rcopy(src, dst, ss, rs, dev):
        return pltpu.make_async_remote_copy(
            src_ref=src, dst_ref=dst, send_sem=ss, recv_sem=rs, device_id=dev, device_id_type=MESH
        )

    barrier = pltpu.get_barrier_semaphore()

    def greet(dev):
        pl.semaphore_signal(barrier, inc=1, device_id=dev, device_id_type=MESH)

    def holder(j):
        return {"col": j // 2, "gz": (j % 2) * 2 + b}

    jz = zl * 2 + zhi
    ypeers = [{"col": ((y + o) % 4) * 4 + zl} for o in range(1, 4)]
    for o in range(1, 4):
        greet({"row": (r + o) % 4})
    for dev in ypeers:
        greet(dev)
    for o in range(1, 8):
        j = (jz + o) % 8
        greet({"col": y * 4 + j // 2, "gz": (j % 2) * 2 + b})
    greet({"gz": zhi * 2 + 1 - b})
    greet({"gz": (1 - zhi) * 2 + 1 - b})
    wraps = ((zl == 0) & (c > 0), (zl == 3) & (c < 15))
    for d in range(2):
        @pl.when(wraps[d])
        def _(d=d):
            greet(nbid[2 + d])
    peers = 15 + jnp.where(wraps[0], 1, 0) + jnp.where(wraps[1], 1, 0)

    cin = []
    for k in range(4):
        rows = pl.ds(k * 2048, 2048)
        cp = pltpu.make_async_copy(field_hbm.at[rows], v0.at[rows], insem.at[k])
        cp.start()
        cin.append(cp)

    cell = tcell_ref[...]
    chosen_xy = onehot((cell >> 7) == iota((64, 1024), 0))
    chosen_z = onehot((cell & 127) == iota((128, 1024), 0))
    mask = nt(chosen_xy, chosen_z).astype(BF)
    for k in range(4):
        m4[k * 64:(k + 1) * 64, :] = mask
    for n in range(8):
        lane = iota((128, 128), 1) - n * 16
        gg[n * 128:(n + 1) * 128, :] = onehot(lane == (iota((128, 128), 0) >> 3))

    @pl.loop(0, 8)
    def _(k):
        rows = pl.ds(pl.multiple_of(k * 128, 128), 128)
        pbuf[rows, :] = onehot((cell >> 3) == iota((128, 1024), 0) + k * 128)

    for k in range(4):
        cin[k].wait()

        @pl.loop(0, 2)
        def _(i, k=k):
            for n in range(4):
                rows = pl.ds(pl.multiple_of(k * 2048 + i * 1024 + n * 256, 256), 256)
                picked[rows, :] = (v0[rows, :] * m4[...]).astype(F32)

        lanes = [picked[pl.ds(k * 2048 + n, 256, stride=8), :].astype(BF) for n in range(8)]
        cbuf[k * 256:(k + 1) * 256, :] = mm(jnp.concatenate(lanes, axis=1), gg[...])

    for o in range(4):
        cols = pl.multiple_of((((r + o) % 4) * 4 + g) * 1024, 1024)
        pltpu.make_async_copy(sb_hbm.at[:, pl.ds(cols, 1024)], sb.at[o], sbsem).start()
    cld = pltpu.make_async_copy(load_hbm, ld, ldsem)
    cld.start()

    for x in range(8):
        c2[:, x * 128:(x + 1) * 128] = cbuf[pl.ds(x, 128, stride=8), :].astype(BF)
    for h in range(2):
        tr[r, h] = mm(c2[...], pbuf[:, h * 512:(h + 1) * 512]).astype(BF)

    pl.semaphore_wait(barrier, peers)

    def half(who, h, sem, dev):
        return rcopy(tr.at[who, h], tr.at[who, h], ts_s, ts_r.at[sem], {"row": dev})

    to_right = [half(r, 0, 0, right), half(r, 1, 2, right)]
    to_left = [half(r, 0, 2, left), half(r, 1, 1, left)]
    from_left = half(left, 0, 0, right)
    from_right = half(right, 1, 1, left)
    relay_right = half(left, 0, 3, right)
    relay_left = half(right, 1, 3, left)
    from_sides = rcopy(tr.at[far], tr.at[far], ts_s, ts_r.at[2], {"row": right})
    from_far = rcopy(tr.at[far], tr.at[far], ts_s, ts_r.at[3], {"row": right})
    to_right[0].start()
    to_left[1].start()
    to_right[1].start()
    to_left[0].start()
    for dev in ypeers:
        pl.semaphore_signal(round_sem, inc=1, device_id=dev, device_id_type=MESH)

    p, q = iota((64, 128), 0), iota((64, 128), 1)
    d, o = p >> 4, p & 7
    qx, qy = (q >> 3) & 7, q & 7
    hit = jnp.where(
        d < 2,
        jnp.where(qx == d * 7, jnp.where(qy == o, 1.0, 0.0), 0.0),
        jnp.where(qy == (d - 2) * 7, jnp.where(qx == o, 1.0, 0.0), 0.0),
    )
    emat[...] = jnp.where(((p >> 3) & 1) == (q >> 6), hit, 0.0).astype(BF)
    wz[...] = onehot(iota((16, 128), 1) == jnp.where(iota((16, 128), 0) < 2, iota((16, 128), 0) * 127, -1))

    def halo(s, d, k):
        if d < 4:
            rows = pl.ds(pl.multiple_of(k * 128, 128), 128)
            src, dst = fs.at[s, d, rows], hb.at[s, d ^ 1, rows]
        else:
            src, dst = zs.at[s, d - 4, k], zh.at[s, (d ^ 1) - 4, k]
        return rcopy(src, dst, hs_s.at[d], hs_r.at[s % 2, d // 2, k], nbid[d])

    def send_halos(s, k, dirs=(2, 3, 0, 1, 4, 5)):
        for d in dirs:
            @pl.when(exists[d])
            def _(d=d):
                halo(s, d, k).start()

    def wait_halos(s, k):
        for axis in range(3):
            low, high = exists[2 * axis], exists[2 * axis + 1]

            def arrived(first, count, axis=axis):
                sides = pl.ds(first, count)
                if axis < 2:
                    dst = hb.at[s, sides, pl.ds(pl.multiple_of(k * 128, 128), 128)]
                else:
                    dst = zh.at[s, sides, k]
                rcopy(dst, dst, hs_s.at[0], hs_r.at[s % 2, axis, k], {"row": right}).wait_recv()
            base = 2 * axis if axis < 2 else 0

            @pl.when(low & high)
            def _(arrived=arrived, base=base):
                arrived(base, 2)

            @pl.when(low & jnp.logical_not(high))
            def _(arrived=arrived, base=base):
                arrived(base, 1)

            @pl.when(high & jnp.logical_not(low))
            def _(arrived=arrived, base=base):
                arrived(base + 1, 1)

    def faces(s, i, pairs):
        for n, pair in enumerate(pairs):
            f = mm(emat[...], pair).astype(BF)
            for j in range(2):
                rows = pl.ds(pl.multiple_of(i * 128 + n * 32 + j * 16, 16), 16)
                for d in range(4):
                    fs[s, d, rows, :] = f[d * 16:(d + 1) * 16, j * 128:(j + 1) * 128]
            v = jnp.concatenate([pair[:, :128], pair[:, 128:]], axis=0)
            zf = nt(wz[...], v)
            for d in range(2):
                zs[s, d, i, n:n + 1, :] = zf[d:d + 1, :]

    def sweep(s, i, vin, vout, more_rows, cols):
        v = [vin[pl.ds(pl.multiple_of(i * 1024 + n * 128, 128), 128), :] for n in range(8)]
        rid = iota((16, 256), 0)
        lhs = []
        for n in range(2):
            ends = jnp.zeros((16, 256), F32)
            for j in range(2):
                for d in range(2):
                    ends = jnp.where(rid == 2 * j + d, zh[s, d, i, 2 * n + j:2 * n + j + 1, :], ends)
            lhs.append(ends)
        lhs = jnp.concatenate([jnp.concatenate(lhs, axis=1)] + more_rows, axis=0).astype(BF)
        t = tn(lhs, cols)
        wide = [
            jnp.concatenate([jnp.concatenate(v[n:n + 2], axis=0), jnp.concatenate(v[n + 2:n + 4], axis=0)], axis=1)
            for n in (0, 4)
        ]
        z = mm(jnp.concatenate(wide, axis=0), ss[...]) + t
        pairs = []
        for n in range(4):
            sides = []
            for j in range(2):
                rows = pl.ds(pl.multiple_of(i * 128 + n * 32 + j * 16, 16), 16)
                sides.append(jnp.concatenate([v[2 * n + j]] + [hb[s, d, rows, :] for d in range(4)], axis=0))
            xy = mm(ah[...], jnp.concatenate(sides, axis=1))
            new = []
            for j in range(2):
                rows = pl.ds(pl.multiple_of(i * 1024 + (2 * n + j) * 128, 128), 128)
                top = (n // 2) * 256 + j * 128
                acc = xy[:, j * 128:(j + 1) * 128] + z[top:top + 128, (n % 2) * 128:(n % 2 + 1) * 128]
                acc = acc + ld[rows, :].astype(F32)
                fresh = (0.2 * v[2 * n + j].astype(F32) + w4[...] * acc).astype(BF)
                vout[rows, :] = fresh
                new.append(fresh)
            pairs.append(jnp.concatenate(new, axis=1))
        return pairs

    def spread(i, values, places):
        m = mm(values, xall[:, pl.ds(pl.multiple_of(i * 1024, 1024), 1024)])
        m = [m[:, n * 256:(n + 1) * 256] * places for n in range(4)]
        return [jnp.concatenate([m[0], m[2]], axis=1), jnp.concatenate([m[1], m[3]], axis=1)]

    def sweep1(first, last):
        @pl.loop(first, last)
        def _(k):
            wait_halos(0, k)
            faces(1, k, sweep(0, k, v0, v1, [], uu[...]))
            send_halos(1, k)

    @pl.loop(0, GROUPS)
    def _(k):
        v = [v0[pl.ds(pl.multiple_of(k * 1024 + n * 128, 128), 128), :] for n in range(8)]
        faces(0, k, [jnp.concatenate(v[2 * n:2 * n + 2], axis=1) for n in range(4)])
        send_halos(0, k, (2, 3, 4, 5))

    p, q = iota((128, 256), 0), iota((128, 256), 1)
    px, py = (p >> 3) & 7, p & 7
    dx = jnp.abs(px - ((q >> 3) & 7))
    dy = jnp.abs(py - (q & 7))
    inside = jnp.where((p >> 6) == ((q >> 6) & 1), jnp.where(dx + dy == 1, 1.0, 0.0), 0.0)
    d, o = (q >> 4) & 7, q & 7
    hit = jnp.where(
        d < 2,
        jnp.where(px == d * 7, jnp.where(py == o, 1.0, 0.0), 0.0),
        jnp.where(py == (d - 2) * 7, jnp.where(px == o, 1.0, 0.0), 0.0),
    )
    hit = jnp.where(((q >> 3) & 1) == (p >> 6), hit, 0.0)
    ah[...] = jnp.where(q < 128, inside, hit)[:, :192].astype(BF)
    p, q = iota((256, 256), 0), iota((256, 256), 1)
    ss[...] = jnp.where((p >> 7) == (q >> 7), jnp.where(jnp.abs(p - q) == 1, 1.0, 0.0), 0.0).astype(BF)
    p, q = iota((16, 256), 0), iota((16, 256), 1)
    uu[...] = jnp.where(p < 4, jnp.where(q == (p >> 1) * 128 + (p & 1) * 127, 1.0, 0.0), 0.0).astype(BF)

    w = OMEGA / (6.0 + coef_ref[...])
    for k in range(2):
        w4[k * 64:(k + 1) * 64, :] = w

    row8 = iota((8, 128), 0) & 3
    cells = jnp.zeros((8, 128), I32)
    weight = jnp.zeros((8, 128), F32)
    number = iota((64, 128), 0) * 128 + iota((64, 128), 1)
    for k in range(4):
        fc = fcell_ref[k]
        wk = jnp.sum(jnp.where(number == fc, w, 0.0), axis=(0, 1), keepdims=True)
        cells = jnp.where(row8 == k, fc, cells)
        weight = jnp.where(row8 == k, wk, weight)
    cinfo[...] = cells.astype(F32)
    for d in range(6):
        @pl.when(exists[d])
        def _(d=d):
            rcopy(cinfo, cnb.at[d ^ 1], i_s.at[d], i_r.at[d ^ 1], nbid[d]).start()

    for d in range(6):
        @pl.when(jnp.logical_not(exists[d]))
        def _(d=d):
            cnb[d] = jnp.zeros((8, 128), F32)
            gnb[d] = jnp.zeros((8, 128), F32)
            for s in range(3):
                if d < 4:
                    @pl.loop(0, 8)
                    def _(k, s=s):
                        hb[s, d, pl.ds(pl.multiple_of(k * 128, 128), 128), :] = jnp.zeros((128, 128), BF)
                else:
                    zh[s, d - 4] = jnp.zeros((GROUPS, 4, 256), F32)

    @pl.loop(0, 8)
    def _(k):
        at = k * 1024 + iota((128, 1024), 1)
        xall[:, pl.ds(pl.multiple_of(k * 1024, 1024), 1024)] = onehot(iota((128, 1024), 0) == (at >> 6))

    from_left.wait_recv()
    relay_right.start()
    from_right.wait_recv()
    relay_left.start()

    @pl.loop(0, GROUPS)
    def _(k):
        send_halos(0, k, (0, 1))

    cld.wait()
    pltpu.make_async_copy(sb, sb, sbsem).wait()

    def product(o):
        src = (r + o) % 4
        return nt(sb[o, :, 0:512], tr[src, 0]) + nt(sb[o, :, 512:1024], tr[src, 1])

    part[...] = product(0)
    from_sides.wait_recv()
    part[...] += product(3)
    part[...] += product(1)
    from_far.wait_recv()
    total = (part[...] + product(2)).reshape(32, 8, 128)
    low, high = total[:, 0:4, :], total[:, 4:8, :]
    first = b == 0
    cown[...] = jnp.where(first, low, high)
    csend[...] = jnp.where(first, high, low)
    core = rcopy(csend, crecv, c_s, c_r, {"gz": g + 1 - 2 * b})
    core.start()
    sweep1(0, 1)

    core.wait_recv()
    qbuf[...] = cown[...] + crecv[...]
    pl.semaphore_wait(round_sem, 3)
    zrecv[me] = qbuf[me]

    @pl.loop(1, 32)
    def _(o):
        j = (me + o) % 32
        rcopy(qbuf.at[j], zrecv.at[me], z_s, z_r, holder(j)).start()
    sweep1(1, 4)

    for d in range(6):
        @pl.when(exists[d])
        def _(d=d):
            rcopy(cnb.at[d], cnb.at[d], i_s.at[d], i_r.at[d], nbid[d]).wait_recv()
    mine = iota((8, 128), 0) < 4
    lane = iota((8, 256), 1) & 63
    for k in range(7):
        if k == 0:
            tx, ty, tz = cells >> 10, (cells >> 7) & 7, cells & 127
        else:
            ox, oy, oz = OFFS[k - 1]
            other = cnb[k - 1].astype(I32)
            at = jnp.where(mine, cells, other)
            tx = (at >> 10) + jnp.where(mine, ox, 7 * ox)
            ty = ((at >> 7) & 7) + jnp.where(mine, oy, 7 * oy)
            tz = (at & 127) + jnp.where(mine, oz, 127 * oz)
        txy = jnp.where((tx >= 0) & (tx < 8) & (ty >= 0) & (ty < 8), tx * 8 + ty, -1)
        tz = jnp.where((tz >= 0) & (tz < 128), tz, -1)
        spots = jnp.where(jnp.concatenate([txy, txy], axis=1) == lane, 1.0, 0.0)
        cols = jnp.where(tz == iota((8, 128), 1), 1.0, 0.0)
        lmask[k * 8:k * 8 + 8, :] = spots
        zcols[16 + k * 8:24 + k * 8, 0:128] = cols
        zcols[16 + k * 8:24 + k * 8, 128:256] = jnp.zeros((8, 128), F32)
        zcols[72 + k * 8:80 + k * 8, 0:128] = jnp.zeros((8, 128), F32)
        zcols[72 + k * 8:80 + k * 8, 128:256] = cols
        if k == 0:
            zcols3[16:24, 0:128] = cols
            zcols3[16:24, 128:256] = jnp.zeros((8, 128), F32)
            zcols3[24:32, 0:128] = jnp.zeros((8, 128), F32)
            zcols3[24:32, 128:256] = cols
    zcols[0:16, :] = uu[...].astype(F32)
    zcols3[0:16, :] = uu[...].astype(F32)

    most = pl.ds(0, 31)
    zall = rcopy(qbuf.at[most], zrecv.at[most], z_s, z_r, holder((me + 1) % 32))
    zall.wait_recv()
    own = jnp.sum(zrecv[...], axis=0)
    fbuf[...] = own
    own8 = jnp.concatenate([own, own], axis=0)
    gvals = weight * own8
    gbuf[...] = gvals
    for d in range(6):
        @pl.when(exists[d])
        def _(d=d):
            rcopy(gbuf, gnb.at[d ^ 1], g_s.at[d], g_r.at[d ^ 1], nbid[d]).start()
    fall[g] = own
    for o in range(1, 4):
        cp = rcopy(fbuf, fall.at[g], f_s, f_r, {"gz": (g + o) % 4})
        cp.start()
    sweep1(4, 8)

    for d in range(6):
        @pl.when(exists[d])
        def _(d=d):
            rcopy(gnb.at[d], gnb.at[d], g_s.at[d], g_r.at[d], nbid[d]).wait_recv()

    def split(values):
        hi = values.astype(BF).astype(F32)
        return hi, values - hi

    hi, lo = split(1.2 * own8)
    val[0:8, :] = jnp.where(mine, hi, lo)
    for d in range(6):
        val[8 + d * 8:16 + d * 8, :] = jnp.where(mine, gvals, gnb[d])
    hi, lo = split(own8)
    val3[...] = jnp.where(mine, hi, lo)

    @pl.loop(0, GROUPS)
    def _(k):
        wait_halos(1, k)
        rows = spread(k, val[...].astype(BF), lmask[...])
        faces(2, k, sweep(1, k, v1, v2, rows, zcols[...].astype(BF)))
        send_halos(2, k)

    def put(k):
        rows = pl.ds(pl.multiple_of(k * 1024, 1024), 1024)
        return pltpu.make_async_copy(v3.at[rows], out_hbm.at[rows], outsem)

    @pl.loop(0, GROUPS)
    def _(k):
        wait_halos(2, k)
        rows = spread(k, val3[...].astype(BF), lmask[0:8, :])
        sweep(2, k, v2, v3, rows, zcols3[...].astype(BF))
        put(k).start()

    others = pl.ds(0, 3)
    fgot = rcopy(qbuf.at[others], fall.at[others], f_s, f_r, {"gz": (g + 1) % 4})
    fgot.wait_recv()
    sel = jnp.where(iota((32, 128), 1) == g * 32 + iota((32, 128), 0), 1.0, 0.0)
    rows16 = jnp.concatenate([fall[0], fall[1], fall[2], fall[3]], axis=0)
    flux_ref[...] = nt(rows16, sel, precision=lax.Precision.HIGHEST)

    sent = pl.ds(0, 3)
    rcopy(tr.at[sent], tr.at[sent], ts_s, ts_r.at[0], {"row": right}).wait_send()
    for cp in (core, zall, fgot):
        cp.wait_send()
    for d in range(6):
        @pl.when(exists[d])
        def _(d=d):
            rcopy(cinfo, cnb.at[d ^ 1], i_s.at[d], i_r.at[d ^ 1], nbid[d]).wait_send()
            rcopy(gbuf, gnb.at[d ^ 1], g_s.at[d], g_r.at[d ^ 1], nbid[d]).wait_send()
            sent = fs.at[:, d] if d < 4 else zs.at[:, d - 4]
            rcopy(sent, sent, hs_s.at[d], hs_r.at[0, d // 2, 0], nbid[d]).wait_send()
    pltpu.make_async_copy(v3, out_hbm, outsem).wait()


def hand_over(src, dst, held, came, left):
    into = [pltpu.make_async_copy(src.at[pl.ds(k * 1024, 1024)], held.at[k], came.at[k]) for k in range(8)]
    out = [pltpu.make_async_copy(held.at[k], dst.at[pl.ds(k * 1024, 1024)], left.at[k]) for k in range(8)]
    for cp in into:
        cp.start()
    for k in range(8):
        into[k].wait()
        out[k].start()
    for cp in out:
        cp.wait()


def per_device(volume_field, volume_load, coefficient, surface_block, trace_cell, flux_cell):
    side_count, first_span, second_span, third_span = volume_field.shape
    rows = side_count * first_span * second_span
    vm = pltpu.VMEM
    dma = pltpu.SemaphoreType.DMA
    scratch = [
        vm((rows, 128), BF), vm((rows, 128), BF), vm((rows, 128), BF), vm((rows, 128), BF), vm((rows, 128), BF),
        vm((4, 256, 1024), BF), vm((4, 2, 128, 512), BF), vm((128, 128), F32),
        vm((3, 4, 1024, 128), BF), vm((3, 4, 1024, 128), BF), vm((3, 2, GROUPS, 4, 256), F32), vm((3, 2, GROUPS, 4, 256), F32),
        vm((128, 192), BF), vm((64, 128), BF), vm((256, 256), BF), vm((1024, 128), BF),
        vm((16, 128), BF), vm((16, 256), BF), vm((256, 128), BF), vm((rows, 128), F32),
        vm((1024, 128), F32), vm((128, 1024), BF),
        vm((1024, 1024), BF), vm((128, 8192), BF),
        vm((256, 128), F32), vm((32, 4, 128), F32), vm((32, 4, 128), F32), vm((32, 4, 128), F32),
        vm((32, 4, 128), F32), vm((32, 4, 128), F32),
        vm((4, 128), F32), vm((4, 4, 128), F32),
        vm((8, 128), F32), vm((6, 8, 128), F32), vm((8, 128), F32), vm((6, 8, 128), F32),
        vm((56, 256), F32), vm((128, 256), F32), vm((32, 256), F32), vm((56, 128), F32), vm((8, 128), F32),
        dma((4,)), dma, dma, dma, dma((6,)), dma((2, 3, GROUPS)),
        dma, dma((4,)), dma, dma, dma, dma, pltpu.SemaphoreType.REGULAR, dma, dma, dma((6,)), dma((6,)), dma((6,)), dma((6,)),
    ]
    anywhere = pl.BlockSpec(memory_space=pl.ANY)
    outside = pl.BlockSpec(memory_space=pltpu.HBM)
    local = pl.BlockSpec(memory_space=pltpu.VMEM)
    new_field, surface_flux = pl.pallas_call(
        kernel,
        out_shape=(jax.ShapeDtypeStruct((rows, 128), BF), jax.ShapeDtypeStruct((16, 32), F32)),
        in_specs=[outside, outside, local, outside, local, pl.BlockSpec(memory_space=pltpu.SMEM)],
        out_specs=(anywhere, local),
        scratch_shapes=scratch,
        compiler_params=pltpu.CompilerParams(
            collective_id=0, has_side_effects=True, vmem_limit_bytes=60 * 1024 * 1024
        ),
    )(
        volume_field.reshape(rows, 128),
        volume_load.reshape(rows, 128),
        coefficient.reshape(64, 128),
        surface_block,
        trace_cell.reshape(1, 1024),
        flux_cell.reshape(4),
    )
    new_field = pl.pallas_call(
        hand_over,
        out_shape=jax.ShapeDtypeStruct((rows, 128), BF),
        in_specs=[anywhere],
        out_specs=anywhere,
        scratch_shapes=[vm((8, rows // 8, 128), BF), dma((8,)), dma((8,))],
    )(new_field)
    return new_field.reshape(volume_field.shape), surface_flux.T


def solution(mesh):
    in_specs = (
        P(None, "row", "col", "gz"),
        P(None, "row", "col", "gz"),
        P("row", "col", "gz"),
        P("row", "col"),
        P("row", "col", "gz", None),
        P("row", "col", "gz", None),
    )
    out_specs = (P(None, "row", "col", "gz"), P("gz", ("row", "col")))
    return jax.shard_map(
        per_device, mesh=mesh, in_specs=in_specs, out_specs=out_specs, check_vma=False
    )
```

```python
import functools

import jax
import jax.numpy as jnp
from jax import lax
from jax.experimental import pallas as pl
from jax.experimental.pallas import tpu as pltpu
from jax.sharding import PartitionSpec as P

MESH = pl.DeviceIdType.MESH
BF = jnp.bfloat16
F32 = jnp.float32
I32 = jnp.int32
OMEGA = 0.8
GROUPS = 8
OFFS = ((-1, 0, 0), (1, 0, 0), (0, -1, 0), (0, 1, 0), (0, 0, -1), (0, 0, 1))


def iota(shape, dim):
    return lax.broadcasted_iota(I32, shape, dim)


def onehot(cond):
    return jnp.where(cond, 1.0, 0.0).astype(BF)


def nt(a, b, **kw):
    return lax.dot_general(a, b, (((1,), (1,)), ((), ())), preferred_element_type=F32, **kw)


def tn(a, b):
    return lax.dot_general(a, b, (((0,), (0,)), ((), ())), preferred_element_type=F32)


def mm(a, b):
    return jnp.dot(a, b, preferred_element_type=F32)


def kernel(
    field_hbm, load_hbm, coef_hbm, sb_hbm, tcell_hbm, fcell_hbm,
    out_hbm, flux_ref,
    v0, ld, v1, v2, v3, sb, tr, w4, hb, fs, zh, zs,
    ah, emat, ss, gg, wz, uu, m4, picked, cbuf, c2, pbuf, xall,
    part, cown, csend, crecv, qbuf, zrecv, fbuf, fall,
    gbuf, gnb, cinfo, cnb, lmask, zcols, zcols3, val, val3,
    insem, ldsem, sbsem, outsem, hs_s, hs_r, ts_s, ts_r, c_s, c_r, z_s, z_r, round_sem,
    f_s, f_r, g_s, g_r, i_s, i_r, tcell_ref, coef_ref, fcell_ref, small,
):
    r = lax.axis_index("row")
    c = lax.axis_index("col")
    g = lax.axis_index("gz")
    y, zl = c // 4, c % 4
    zhi, b = g // 2, g % 2
    right, left, far = (r + 1) % 4, (r + 3) % 4, (r + 2) % 4
    me = c * 2 + zhi

    exists = (r > 0, r < 3, c > 0, c < 15, g > 0, g < 3)
    nbid = ({"row": r - 1}, {"row": r + 1}, {"col": c - 1}, {"col": c + 1}, {"gz": g - 1}, {"gz": g + 1})

    def rcopy(src, dst, ss, rs, dev):
        return pltpu.make_async_remote_copy(
            src_ref=src, dst_ref=dst, send_sem=ss, recv_sem=rs, device_id=dev, device_id_type=MESH
        )

    count = sum(jnp.where(e, 1, 0) for e in exists)

    def beside(ref, ss, rs, receive):
        for n in range(3, 7):
            @pl.when(count == n)
            def _(n=n):
                some = ref.at[pl.ds(0, n)]
                cp = rcopy(some, some, ss, rs, {"row": right})
                if receive:
                    cp.wait_recv()
                else:
                    cp.wait_send()

    smalls = [
        pltpu.make_async_copy(tcell_hbm, tcell_ref, small.at[0]),
        pltpu.make_async_copy(coef_hbm, coef_ref, small.at[1]),
        pltpu.make_async_copy(fcell_hbm, fcell_ref, small.at[2]),
    ]
    for cp in smalls:
        cp.start()
    barrier = pltpu.get_barrier_semaphore()

    def greet(dev):
        pl.semaphore_signal(barrier, inc=1, device_id=dev, device_id_type=MESH)

    def holder(j):
        return {"col": j // 2, "gz": (j % 2) * 2 + b}

    jz = zl * 2 + zhi
    ypeers = [{"col": ((y + o) % 4) * 4 + zl} for o in range(1, 4)]
    for o in range(1, 4):
        greet({"row": (r + o) % 4})
    for dev in ypeers:
        greet(dev)
    for o in range(1, 8):
        j = (jz + o) % 8
        greet({"col": y * 4 + j // 2, "gz": (j % 2) * 2 + b})
    greet({"gz": zhi * 2 + 1 - b})
    greet({"gz": (1 - zhi) * 2 + 1 - b})
    wraps = ((zl == 0) & (c > 0), (zl == 3) & (c < 15))
    for d in range(2):
        @pl.when(wraps[d])
        def _(d=d):
            greet(nbid[2 + d])
    peers = 15 + jnp.where(wraps[0], 1, 0) + jnp.where(wraps[1], 1, 0)

    cin = []
    for k in range(4):
        rows = pl.ds(k * 2048, 2048)
        cp = pltpu.make_async_copy(field_hbm.at[rows], v0.at[rows], insem.at[k])
        cp.start()
        cin.append(cp)

    smalls[0].wait()
    cell = tcell_ref[...]
    chosen_xy = onehot((cell >> 7) == iota((64, 1024), 0))
    chosen_z = onehot((cell & 127) == iota((128, 1024), 0))
    mask = nt(chosen_xy, chosen_z).astype(BF)
    for k in range(4):
        m4[k * 64:(k + 1) * 64, :] = mask
    for n in range(8):
        lane = iota((128, 128), 1) - n * 16
        gg[n * 128:(n + 1) * 128, :] = onehot(lane == (iota((128, 128), 0) >> 3))

    @pl.loop(0, 8)
    def _(k):
        rows = pl.ds(pl.multiple_of(k * 128, 128), 128)
        pbuf[rows, :] = onehot((cell >> 3) == iota((128, 1024), 0) + k * 128)

    for k in range(4):
        cin[k].wait()

        @pl.loop(0, 2)
        def _(i, k=k):
            for n in range(4):
                rows = pl.ds(pl.multiple_of(k * 2048 + i * 1024 + n * 256, 256), 256)
                picked[rows, :] = (v0[rows, :] * m4[...]).astype(F32)

        lanes = [picked[pl.ds(k * 2048 + n, 256, stride=8), :].astype(BF) for n in range(8)]
        cbuf[k * 256:(k + 1) * 256, :] = mm(jnp.concatenate(lanes, axis=1), gg[...])

    for o in range(4):
        cols = pl.multiple_of((((r + o) % 4) * 4 + g) * 1024, 1024)
        pltpu.make_async_copy(sb_hbm.at[:, pl.ds(cols, 1024)], sb.at[o], sbsem).start()
    cld = pltpu.make_async_copy(load_hbm, ld, ldsem)
    cld.start()

    for x in range(8):
        c2[:, x * 128:(x + 1) * 128] = cbuf[pl.ds(x, 128, stride=8), :].astype(BF)
    for h in range(2):
        tr[r, h] = mm(c2[...], pbuf[:, h * 512:(h + 1) * 512]).astype(BF)

    pl.semaphore_wait(barrier, peers)

    def half(who, h, sem, dev):
        return rcopy(tr.at[who, h], tr.at[who, h], ts_s, ts_r.at[sem], {"row": dev})

    to_right = [half(r, 0, 0, right), half(r, 1, 2, right)]
    to_left = [half(r, 0, 2, left), half(r, 1, 1, left)]
    from_left = half(left, 0, 0, right)
    from_right = half(right, 1, 1, left)
    relay_right = half(left, 0, 3, right)
    relay_left = half(right, 1, 3, left)
    from_sides = rcopy(tr.at[far], tr.at[far], ts_s, ts_r.at[2], {"row": right})
    from_far = rcopy(tr.at[far], tr.at[far], ts_s, ts_r.at[3], {"row": right})
    to_right[0].start()
    to_left[1].start()
    to_right[1].start()
    to_left[0].start()
    for dev in ypeers:
        pl.semaphore_signal(round_sem, inc=1, device_id=dev, device_id_type=MESH)

    p, q = iota((64, 128), 0), iota((64, 128), 1)
    d, o = p >> 4, p & 7
    qx, qy = (q >> 3) & 7, q & 7
    hit = jnp.where(
        d < 2,
        jnp.where(qx == d * 7, jnp.where(qy == o, 1.0, 0.0), 0.0),
        jnp.where(qy == (d - 2) * 7, jnp.where(qx == o, 1.0, 0.0), 0.0),
    )
    emat[...] = jnp.where(((p >> 3) & 1) == (q >> 6), hit, 0.0).astype(BF)
    wz[...] = onehot(iota((16, 128), 1) == jnp.where(iota((16, 128), 0) < 2, iota((16, 128), 0) * 127, -1))

    def halo(s, d, k):
        if d < 4:
            rows = pl.ds(pl.multiple_of(k * 128, 128), 128)
            src, dst = fs.at[s, d, rows], hb.at[s, d ^ 1, rows]
        else:
            src, dst = zs.at[s, d - 4, k], zh.at[s, (d ^ 1) - 4, k]
        return rcopy(src, dst, hs_s.at[d], hs_r.at[s % 2, d // 2, k], nbid[d])

    def send_halos(s, k, dirs=(2, 3, 0, 1, 4, 5)):
        for d in dirs:
            @pl.when(exists[d])
            def _(d=d):
                halo(s, d, k).start()

    def wait_halos(s, k):
        for axis in range(3):
            low, high = exists[2 * axis], exists[2 * axis + 1]

            def arrived(first, count, axis=axis):
                sides = pl.ds(first, count)
                if axis < 2:
                    dst = hb.at[s, sides, pl.ds(pl.multiple_of(k * 128, 128), 128)]
                else:
                    dst = zh.at[s, sides, k]
                rcopy(dst, dst, hs_s.at[0], hs_r.at[s % 2, axis, k], {"row": right}).wait_recv()
            base = 2 * axis if axis < 2 else 0

            @pl.when(low & high)
            def _(arrived=arrived, base=base):
                arrived(base, 2)

            @pl.when(low & jnp.logical_not(high))
            def _(arrived=arrived, base=base):
                arrived(base, 1)

            @pl.when(high & jnp.logical_not(low))
            def _(arrived=arrived, base=base):
                arrived(base + 1, 1)

    def faces(s, i, pairs):
        edge = ([], [])
        for n, pair in enumerate(pairs):
            f = mm(emat[...], pair).astype(BF)
            for j in range(2):
                rows = pl.ds(pl.multiple_of(i * 128 + n * 32 + j * 16, 16), 16)
                for d in range(4):
                    fs[s, d, rows, :] = f[d * 16:(d + 1) * 16, j * 128:(j + 1) * 128]
            v = jnp.concatenate([pair[:, :128], pair[:, 128:]], axis=0)
            zf = nt(wz[...], v)
            for d in range(2):
                edge[d].extend([zf[d:d + 1, :128], zf[d:d + 1, 128:]])
        for d in range(2):
            zs[s, d, i] = jnp.concatenate(edge[d], axis=0).astype(BF)

    def sweep(s, i, vin, vout, more_rows, cols):
        v = [vin[pl.ds(pl.multiple_of(i * 1024 + n * 128, 128), 128), :] for n in range(8)]
        rid = iota((16, 256), 0)
        edge = [zh[s, d, i].astype(F32) for d in range(2)]
        lhs = []
        for n in range(2):
            ends = jnp.zeros((16, 256), F32)
            for j in range(2):
                for d in range(2):
                    at = 4 * n + 2 * j
                    row = jnp.concatenate([edge[d][at:at + 1, :], edge[d][at + 1:at + 2, :]], axis=1)
                    ends = jnp.where(rid == 2 * j + d, row, ends)
            lhs.append(ends)
        lhs = jnp.concatenate([jnp.concatenate(lhs, axis=1)] + more_rows, axis=0).astype(BF)
        t = tn(lhs, cols)
        wide = [
            jnp.concatenate([jnp.concatenate(v[n:n + 2], axis=0), jnp.concatenate(v[n + 2:n + 4], axis=0)], axis=1)
            for n in (0, 4)
        ]
        z = mm(jnp.concatenate(wide, axis=0), ss[...]) + t
        pairs = []
        for n in range(4):
            sides = []
            for j in range(2):
                rows = pl.ds(pl.multiple_of(i * 128 + n * 32 + j * 16, 16), 16)
                sides.append(jnp.concatenate([v[2 * n + j]] + [hb[s, d, rows, :] for d in range(4)], axis=0))
            xy = mm(ah[...], jnp.concatenate(sides, axis=1))
            new = []
            for j in range(2):
                rows = pl.ds(pl.multiple_of(i * 1024 + (2 * n + j) * 128, 128), 128)
                top = (n // 2) * 256 + j * 128
                acc = xy[:, j * 128:(j + 1) * 128] + z[top:top + 128, (n % 2) * 128:(n % 2 + 1) * 128]
                acc = acc + ld[rows, :].astype(F32)
                fresh = (0.2 * v[2 * n + j].astype(F32) + w4[...] * acc).astype(BF)
                vout[rows, :] = fresh
                new.append(fresh)
            pairs.append(jnp.concatenate(new, axis=1))
        return pairs

    def spread(i, values, places):
        m = mm(values, xall[:, pl.ds(pl.multiple_of(i * 1024, 1024), 1024)])
        m = [m[:, n * 256:(n + 1) * 256] * places for n in range(4)]
        return [jnp.concatenate([m[0], m[2]], axis=1), jnp.concatenate([m[1], m[3]], axis=1)]

    def sweep1(first, last):
        @pl.loop(first, last)
        def _(k):
            wait_halos(0, k)
            faces(1, k, sweep(0, k, v0, v1, [], uu[...]))
            send_halos(1, k)

    @pl.loop(0, GROUPS)
    def _(k):
        v = [v0[pl.ds(pl.multiple_of(k * 1024 + n * 128, 128), 128), :] for n in range(8)]
        faces(0, k, [jnp.concatenate(v[2 * n:2 * n + 2], axis=1) for n in range(4)])
        send_halos(0, k, (2, 3, 4, 5))

    p, q = iota((128, 256), 0), iota((128, 256), 1)
    px, py = (p >> 3) & 7, p & 7
    dx = jnp.abs(px - ((q >> 3) & 7))
    dy = jnp.abs(py - (q & 7))
    inside = jnp.where((p >> 6) == ((q >> 6) & 1), jnp.where(dx + dy == 1, 1.0, 0.0), 0.0)
    d, o = (q >> 4) & 7, q & 7
    hit = jnp.where(
        d < 2,
        jnp.where(px == d * 7, jnp.where(py == o, 1.0, 0.0), 0.0),
        jnp.where(py == (d - 2) * 7, jnp.where(px == o, 1.0, 0.0), 0.0),
    )
    hit = jnp.where(((q >> 3) & 1) == (p >> 6), hit, 0.0)
    ah[...] = jnp.where(q < 128, inside, hit)[:, :192].astype(BF)
    p, q = iota((256, 256), 0), iota((256, 256), 1)
    ss[...] = jnp.where((p >> 7) == (q >> 7), jnp.where(jnp.abs(p - q) == 1, 1.0, 0.0), 0.0).astype(BF)
    p, q = iota((16, 256), 0), iota((16, 256), 1)
    uu[...] = jnp.where(p < 4, jnp.where(q == (p >> 1) * 128 + (p & 1) * 127, 1.0, 0.0), 0.0).astype(BF)

    smalls[1].wait()
    smalls[2].wait()
    w = OMEGA / (6.0 + coef_ref[...])
    for k in range(2):
        w4[k * 64:(k + 1) * 64, :] = w

    row8 = iota((8, 128), 0) & 3
    cells = jnp.zeros((8, 128), I32)
    weight = jnp.zeros((8, 128), F32)
    number = iota((64, 128), 0) * 128 + iota((64, 128), 1)
    for k in range(4):
        fc = fcell_ref[k]
        wk = jnp.sum(jnp.where(number == fc, w, 0.0), axis=(0, 1), keepdims=True)
        cells = jnp.where(row8 == k, fc, cells)
        weight = jnp.where(row8 == k, wk, weight)
    cinfo[...] = cells.astype(F32)
    for d in range(6):
        @pl.when(exists[d])
        def _(d=d):
            rcopy(cinfo, cnb.at[d ^ 1], i_s, i_r, nbid[d]).start()

    for d in range(6):
        @pl.when(jnp.logical_not(exists[d]))
        def _(d=d):
            cnb[d] = jnp.zeros((8, 128), F32)
            gnb[d] = jnp.zeros((8, 128), F32)
            for s in range(3):
                if d < 4:
                    @pl.loop(0, 8)
                    def _(k, s=s):
                        hb[s, d, pl.ds(pl.multiple_of(k * 128, 128), 128), :] = jnp.zeros((128, 128), BF)
                else:
                    zh[s, d - 4] = jnp.zeros((GROUPS, 8, 128), BF)

    @pl.loop(0, 8)
    def _(k):
        at = k * 1024 + iota((128, 1024), 1)
        xall[:, pl.ds(pl.multiple_of(k * 1024, 1024), 1024)] = onehot(iota((128, 1024), 0) == (at >> 6))

    from_left.wait_recv()
    relay_right.start()
    from_right.wait_recv()
    relay_left.start()

    @pl.loop(0, GROUPS)
    def _(k):
        send_halos(0, k, (0, 1))

    cld.wait()
    pltpu.make_async_copy(sb, sb, sbsem).wait()

    def product(o):
        src = (r + o) % 4
        return nt(sb[o, :, 0:512], tr[src, 0]) + nt(sb[o, :, 512:1024], tr[src, 1])

    part[...] = product(0)
    from_sides.wait_recv()
    part[...] += product(3)
    part[...] += product(1)
    from_far.wait_recv()
    total = (part[...] + product(2)).reshape(32, 8, 128)
    low, high = total[:, 0:4, :], total[:, 4:8, :]
    first = b == 0
    cown[...] = jnp.where(first, low, high)
    csend[...] = jnp.where(first, high, low)
    core = rcopy(csend, crecv, c_s, c_r, {"gz": g + 1 - 2 * b})
    core.start()
    sweep1(0, 1)

    core.wait_recv()
    qbuf[...] = cown[...] + crecv[...]
    pl.semaphore_wait(round_sem, 3)
    zrecv[me] = qbuf[me]

    @pl.loop(1, 32)
    def _(o):
        j = (me + o) % 32
        rcopy(qbuf.at[j], zrecv.at[me], z_s, z_r, holder(j)).start()
    sweep1(1, 4)

    beside(cnb, i_s, i_r, True)
    mine = iota((8, 128), 0) < 4
    lane = iota((8, 256), 1) & 63
    for k in range(7):
        if k == 0:
            tx, ty, tz = cells >> 10, (cells >> 7) & 7, cells & 127
        else:
            ox, oy, oz = OFFS[k - 1]
            other = cnb[k - 1].astype(I32)
            at = jnp.where(mine, cells, other)
            tx = (at >> 10) + jnp.where(mine, ox, 7 * ox)
            ty = ((at >> 7) & 7) + jnp.where(mine, oy, 7 * oy)
            tz = (at & 127) + jnp.where(mine, oz, 127 * oz)
        txy = jnp.where((tx >= 0) & (tx < 8) & (ty >= 0) & (ty < 8), tx * 8 + ty, -1)
        tz = jnp.where((tz >= 0) & (tz < 128), tz, -1)
        spots = jnp.where(jnp.concatenate([txy, txy], axis=1) == lane, 1.0, 0.0)
        cols = jnp.where(tz == iota((8, 128), 1), 1.0, 0.0)
        lmask[k * 8:k * 8 + 8, :] = spots
        zcols[16 + k * 8:24 + k * 8, 0:128] = cols
        zcols[16 + k * 8:24 + k * 8, 128:256] = jnp.zeros((8, 128), F32)
        zcols[72 + k * 8:80 + k * 8, 0:128] = jnp.zeros((8, 128), F32)
        zcols[72 + k * 8:80 + k * 8, 128:256] = cols
        if k == 0:
            zcols3[16:24, 0:128] = cols
            zcols3[16:24, 128:256] = jnp.zeros((8, 128), F32)
            zcols3[24:32, 0:128] = jnp.zeros((8, 128), F32)
            zcols3[24:32, 128:256] = cols
    zcols[0:16, :] = uu[...].astype(F32)
    zcols3[0:16, :] = uu[...].astype(F32)

    most = pl.ds(0, 31)
    zall = rcopy(qbuf.at[most], zrecv.at[most], z_s, z_r, holder((me + 1) % 32))
    zall.wait_recv()
    own = jnp.sum(zrecv[...], axis=0)
    fbuf[...] = own
    own8 = jnp.concatenate([own, own], axis=0)
    gvals = weight * own8
    gbuf[...] = gvals
    for d in range(6):
        @pl.when(exists[d])
        def _(d=d):
            rcopy(gbuf, gnb.at[d ^ 1], g_s, g_r, nbid[d]).start()
    fall[g] = own
    for o in range(1, 4):
        cp = rcopy(fbuf, fall.at[g], f_s, f_r, {"gz": (g + o) % 4})
        cp.start()
    sweep1(4, 8)

    beside(gnb, g_s, g_r, True)

    def split(values):
        hi = values.astype(BF).astype(F32)
        return hi, values - hi

    hi, lo = split(1.2 * own8)
    val[0:8, :] = jnp.where(mine, hi, lo)
    for d in range(6):
        val[8 + d * 8:16 + d * 8, :] = jnp.where(mine, gvals, gnb[d])
    hi, lo = split(own8)
    val3[...] = jnp.where(mine, hi, lo)

    @pl.loop(0, GROUPS)
    def _(k):
        wait_halos(1, k)
        rows = spread(k, val[...].astype(BF), lmask[...])
        faces(2, k, sweep(1, k, v1, v2, rows, zcols[...].astype(BF)))
        send_halos(2, k)

    others = pl.ds(0, 3)
    fgot = rcopy(qbuf.at[others], fall.at[others], f_s, f_r, {"gz": (g + 1) % 4})
    fgot.wait_recv()
    sel = jnp.where(iota((32, 128), 1) == g * 32 + iota((32, 128), 0), 1.0, 0.0)
    rows16 = jnp.concatenate([fall[0], fall[1], fall[2], fall[3]], axis=0)
    flux_ref[...] = nt(rows16, sel, precision=lax.Precision.HIGHEST)

    def put(k):
        rows = pl.ds(pl.multiple_of(k * 1024, 1024), 1024)
        return pltpu.make_async_copy(v3.at[rows], out_hbm.at[rows], outsem)

    @pl.loop(0, GROUPS)
    def _(k):
        wait_halos(2, k)
        rows = spread(k, val3[...].astype(BF), lmask[0:8, :])
        sweep(2, k, v2, v3, rows, zcols3[...].astype(BF))
        put(k).start()

    beside(cnb, i_s, i_r, False)
    beside(gnb, g_s, g_r, False)
    sent = pl.ds(0, 3)
    rcopy(tr.at[sent], tr.at[sent], ts_s, ts_r.at[0], {"row": right}).wait_send()
    for cp in (core, zall, fgot):
        cp.wait_send()
    for d in range(6):
        @pl.when(exists[d])
        def _(d=d):
            sent = fs.at[:, d] if d < 4 else zs.at[:, d - 4]
            rcopy(sent, sent, hs_s.at[d], hs_r.at[0, d // 2, 0], nbid[d]).wait_send()
    pltpu.make_async_copy(v3, out_hbm, outsem).wait()


def hand_over(src, flux, dst, flux_out, held, small, came, left, sides):
    into = [pltpu.make_async_copy(src.at[pl.ds(k * 1024, 1024)], held.at[k], came.at[k]) for k in range(8)]
    for cp in into:
        cp.start()
    first = pltpu.make_async_copy(flux, small, sides.at[0])
    second = pltpu.make_async_copy(small, flux_out, sides.at[1])
    first.start()
    for k in range(8):
        into[k].wait()
        pltpu.make_async_copy(held.at[k], dst.at[pl.ds(k * 1024, 1024)], left).start()
    first.wait()
    second.start()
    pltpu.make_async_copy(src, dst, left).wait()
    second.wait()


def per_device(volume_field, volume_load, coefficient, surface_block, trace_cell, flux_cell):
    side_count, first_span, second_span, third_span = volume_field.shape
    rows = side_count * first_span * second_span
    vm = pltpu.VMEM
    dma = pltpu.SemaphoreType.DMA
    scratch = [
        vm((rows, 128), BF), vm((rows, 128), BF), vm((rows, 128), BF), vm((rows, 128), BF), vm((rows, 128), BF),
        vm((4, 256, 1024), BF), vm((4, 2, 128, 512), BF), vm((128, 128), F32),
        vm((3, 4, 1024, 128), BF), vm((3, 4, 1024, 128), BF), vm((3, 2, GROUPS, 8, 128), BF), vm((3, 2, GROUPS, 8, 128), BF),
        vm((128, 192), BF), vm((64, 128), BF), vm((256, 256), BF), vm((1024, 128), BF),
        vm((16, 128), BF), vm((16, 256), BF), vm((256, 128), BF), vm((rows, 128), F32),
        vm((1024, 128), F32), vm((128, 1024), BF),
        vm((1024, 1024), BF), vm((128, 8192), BF),
        vm((256, 128), F32), vm((32, 4, 128), F32), vm((32, 4, 128), F32), vm((32, 4, 128), F32),
        vm((32, 4, 128), F32), vm((32, 4, 128), F32),
        vm((4, 128), F32), vm((4, 4, 128), F32),
        vm((8, 128), F32), vm((6, 8, 128), F32), vm((8, 128), F32), vm((6, 8, 128), F32),
        vm((56, 256), F32), vm((128, 256), F32), vm((32, 256), F32), vm((56, 128), F32), vm((8, 128), F32),
        dma((4,)), dma, dma, dma, dma((6,)), dma((2, 3, GROUPS)),
        dma, dma((4,)), dma, dma, dma, dma, pltpu.SemaphoreType.REGULAR, dma, dma, dma, dma, dma, dma,
        vm((1, 1024), I32), vm((64, 128), F32), pltpu.SMEM((4,), I32), dma((3,)),
    ]
    anywhere = pl.BlockSpec(memory_space=pl.ANY)
    outside = pl.BlockSpec(memory_space=pltpu.HBM)
    local = pl.BlockSpec(memory_space=pltpu.VMEM)
    new_field, surface_flux = pl.pallas_call(
        kernel,
        out_shape=(jax.ShapeDtypeStruct((rows, 128), BF), jax.ShapeDtypeStruct((16, 32), F32)),
        in_specs=[anywhere] * 6,
        out_specs=(anywhere, local),
        scratch_shapes=scratch,
        compiler_params=pltpu.CompilerParams(
            collective_id=0, has_side_effects=True, vmem_limit_bytes=60 * 1024 * 1024
        ),
    )(
        volume_field.reshape(rows, 128),
        volume_load.reshape(rows, 128),
        coefficient.reshape(64, 128),
        surface_block,
        trace_cell.reshape(1, 1024),
        flux_cell.reshape(4),
    )
    new_field, surface_flux = pl.pallas_call(
        hand_over,
        out_shape=(jax.ShapeDtypeStruct((rows, 128), BF), jax.ShapeDtypeStruct((16, 32), F32)),
        in_specs=[anywhere, anywhere],
        out_specs=(anywhere, anywhere),
        scratch_shapes=[vm((8, rows // 8, 128), BF), vm((16, 32), F32), dma((8,)), dma, dma((2,))],
    )(new_field, surface_flux)
    return new_field.reshape(volume_field.shape), surface_flux.T


def solution(mesh):
    in_specs = (
        P(None, "row", "col", "gz"),
        P(None, "row", "col", "gz"),
        P("row", "col", "gz"),
        P("row", "col"),
        P("row", "col", "gz", None),
        P("row", "col", "gz", None),
    )
    out_specs = (P(None, "row", "col", "gz"), P("gz", ("row", "col")))
    return jax.shard_map(
        per_device, mesh=mesh, in_specs=in_specs, out_specs=out_specs, check_vma=False
    )
```
